256 devices in a mesh: leaf: 256 (over x, z, y, core).
Axes of the slice: x: 4, y: 4, z: 8, core: 2. Of those that a mesh axis runs over, the one named last changes fastest.
Arguments:
- points: bfloat16 [128, 2097152], P(None, 'leaf')
- probes: bfloat16 [16, 2097152], P(None, 'leaf'), may hold values from -6 to 6
- near_list: int32 [4096, 4], P('leaf'), may hold values from 0 to 4095, as said below
- near_count: int32 [4096], P('leaf'), may hold values from 1 to 4, as said below
- leaf_skel: int32 [4096, 128], P('leaf'), may hold values from 0 to 511, as said below
- local_skel: int32 [3840, 128], P('leaf'), may hold values from 0 to 255, as said below
- upper_skel: int32 [255, 128], replicated, may hold values from 0 to 255, as said below
Outputs:
- response: float32 [16, 2097152], P(None, 'leaf')
The draws below stay inside these ranges and needn't reach their ends.
Inputs may be any that keep to these rules, and one draw needn't show every extreme that they name: `near_list`: entry 0 of leaf t's list is t itself; every entry is a leaf of the same block of 16 consecutive leaves as t, or of the block just before or just after it. `near_count`: some leaf uses all 4 slots. `leaf_skel`: each row holds 128 distinct values. `local_skel`: each row holds 128 distinct values. `upper_skel`: each row holds 128 distinct values.
All inputs are finite; a program needn't handle non-finite values.
Results may differ from the reference program's by a relative error of at most 0.0015.
Values may be sent and summed in bfloat16 or wider, within the bound.
No kernel may reach another device: no remote copies, remote signals or barrier semaphores. Data moves between devices by JAX's collectives and lax.ppermute only.
A program may use at most 128 MiB of HBM per device.

```python
import jax
import jax.numpy as jnp
from jax import lax

D = 128
PROBES = 16
LEAF = 512
SKEL = 128
NEAR = 4
LOC_LEVELS = 4
LEAF_DEV = 16
LEAVES = 4096
POINTS = 2097152
LOCAL_NODES = 3840
UPPER_NODES = 255
N_LEAF = 256


def draw_points(key, part):
    shape = (D, POINTS)
    values = jax.random.normal(key, shape, jnp.float32)
    return values.astype(jnp.bfloat16)


def near_tables(key):
    base = jax.random.fold_in(key, 11)
    key_dev, key_leaf, key_top, key_count = jax.random.split(base, 4)
    leaf_ids = jnp.arange(LEAVES, dtype=jnp.int32)
    group_of = leaf_ids // LEAF_DEV
    group_num = LEAVES // LEAF_DEV
    hop_dir = jax.random.randint(key_dev, (LEAVES, NEAR), -1, 2, dtype=jnp.int32)
    src_group = jnp.clip(group_of[:, None] + hop_dir, 0, group_num - 1)
    src_leaf = jax.random.randint(key_leaf, (LEAVES, NEAR), 0, LEAF_DEV, dtype=jnp.int32)
    listed = src_group * LEAF_DEV + src_leaf
    before_group = jnp.where(group_of > 0, group_of - 1, group_of + 1)
    after_group = jnp.where(group_of < group_num - 1, group_of + 1, group_of - 1)
    listed = listed.at[:, 1].set(before_group * LEAF_DEV + src_leaf[:, 1])
    listed = listed.at[:, 2].set(after_group * LEAF_DEV + src_leaf[:, 2])
    listed = listed.at[:, 0].set(leaf_ids)
    ceiling = jax.random.randint(key_top, (group_num,), 2, NEAR + 1, dtype=jnp.int32)[group_of]
    counts = jax.random.randint(key_count, (LEAVES,), 1, ceiling + 1, dtype=jnp.int32)
    counts = jnp.where(leaf_ids % LEAF_DEV == 0, NEAR, counts).astype(jnp.int32)
    return (listed.astype(jnp.int32), counts)


def draw_near_list(key, part):
    return near_tables(key)[0]


def draw_near_count(key, part):
    return near_tables(key)[1]


def pick_rows(key, row_num, pool):
    row_keys = jax.random.split(key, row_num)
    picked = jax.vmap(lambda row_key: jax.random.permutation(row_key, pool)[:SKEL])(row_keys)
    return picked.astype(jnp.int32)


def draw_leaf_skel(key, part):
    return pick_rows(jax.random.fold_in(key, 21), LEAVES, LEAF)


def draw_local_skel(key, part):
    return pick_rows(jax.random.fold_in(key, 22), LOCAL_NODES, 2 * SKEL)


def draw_upper_skel(key, part):
    return pick_rows(jax.random.fold_in(key, 23), UPPER_NODES, 2 * SKEL)


def shard_levels(rng, extent, shards, least, largest):
    def one(dim, shards_of):
        draws = jax.random.uniform(jax.random.fold_in(jax.random.fold_in(rng, 6), dim), (shards_of,), jnp.float32, least / len(shards), largest / len(shards))
        return jnp.repeat(jnp.exp(draws), extent[dim] // shards_of).reshape((-1,) + (1,) * (len(extent) - dim - 1))

    loudness = one(*shards[0])
    for cut in shards[1:]:
        loudness = loudness * one(*cut)
    return loudness


def scatter_about(rng, shape, width, limit, shards=(), held_as=jnp.bfloat16):
    array = jax.random.normal(rng, shape, jnp.float32) * width
    if len(shards) > 0:
        array = shard_levels(rng, shape, shards, -0.22, 0.18) * array
    return jnp.clip(array, min=-limit, max=limit).astype(held_as)


def setup_inputs(seed: int = 0) -> dict:
    key_list = jax.random.split(jax.random.key(seed), 8)
    points = draw_points(jax.random.fold_in(key_list[7], 71), 0)
    probes = scatter_about(key_list[1], (PROBES, POINTS), 1.0, 6.0, ((1, 256),))
    near_list = draw_near_list(jax.random.fold_in(key_list[7], 71), 0)
    near_count = draw_near_count(jax.random.fold_in(key_list[7], 71), 0)
    leaf_skel = draw_leaf_skel(jax.random.fold_in(key_list[7], 71), 0)
    local_skel = draw_local_skel(jax.random.fold_in(key_list[7], 71), 0)
    upper_skel = draw_upper_skel(jax.random.fold_in(key_list[7], 71), 0)
    return {"points": points, "probes": probes, "near_list": near_list, "near_count": near_count, "leaf_skel": leaf_skel, "local_skel": local_skel, "upper_skel": upper_skel}


HIGH = lax.Precision.HIGHEST


def kernel_block(left_pts, right_pts):
    left_wide = left_pts.astype(jnp.float32)
    right_wide = right_pts.astype(jnp.float32)
    left_sq = jnp.sum(left_wide * left_wide, axis=0)
    right_sq = jnp.sum(right_wide * right_wide, axis=0)
    inner_prod = jnp.dot(left_wide.T, right_wide, precision=HIGH)
    distance = left_sq[:, None] + right_sq[None, :] - 2.0 * inner_prod
    return jnp.exp(distance * (-2.0 / left_pts.shape[0]))


def kernel_batch(left_pts, right_pts):
    return jax.vmap(kernel_block)(left_pts, right_pts)


def up_level(child_pts, child_q, chosen):
    node_num, skel_len = chosen.shape
    emb_width = child_pts.shape[1]
    probe_num = child_q.shape[1]
    paired_pts = child_pts.reshape(node_num, 2, emb_width, skel_len)
    paired_q = child_q.reshape(node_num, 2, probe_num, skel_len).astype(jnp.float32)
    first_pts = paired_pts[:, 0]
    second_pts = paired_pts[:, 1]
    first_q = paired_q[:, 0]
    second_q = paired_q[:, 1]
    cross_k = kernel_batch(first_pts, second_pts)
    couple_first = jnp.einsum("npj,nij->npi", second_q, cross_k, precision=HIGH)
    couple_second = jnp.einsum("npi,nij->npj", first_q, cross_k, precision=HIGH)
    coupling = jnp.stack([couple_first, couple_second], axis=1).reshape(2 * node_num, probe_num, skel_len)
    joined_pts = jnp.concatenate([first_pts, second_pts], axis=2)
    joined_q = jnp.concatenate([first_q, second_q], axis=2)
    parent_pts = jnp.take_along_axis(joined_pts, chosen[:, None, :], axis=2)
    up_kernel = kernel_batch(joined_pts, parent_pts)
    parent_q = jnp.einsum("npc,ncs->nps", joined_q, up_kernel, precision=HIGH).astype(jnp.bfloat16)
    return parent_pts, parent_q, up_kernel, coupling


def descend(down_field, up_kernel, coupling):
    node_num, probe_num, skel_len = down_field.shape
    spread = jnp.einsum("nps,ncs->npc", down_field, up_kernel, precision=HIGH)
    spread = spread.reshape(node_num, probe_num, 2, skel_len).transpose(0, 2, 1, 3)
    return spread.reshape(2 * node_num, probe_num, skel_len) + coupling


def reference(points, probes, near_list, near_count, leaf_skel, local_skel, upper_skel):
    leaf_tiles = points.reshape(D, LEAVES, LEAF)
    probe_tiles = probes.reshape(PROBES, LEAVES, LEAF)
    leaf_ids = jnp.arange(LEAVES, dtype=jnp.int32)

    def near_leaf(leaf_id):
        target = leaf_tiles[:, leaf_id]
        sources = near_list[leaf_id]
        src_pts = jnp.take(leaf_tiles, sources, axis=1)
        src_prb = jnp.take(probe_tiles, sources, axis=1).astype(jnp.float32)
        blocks = jax.vmap(kernel_block, in_axes=(None, 1))(target, src_pts)
        blocks = lax.optimization_barrier(blocks.astype(jnp.bfloat16)).astype(jnp.float32)
        contrib = jnp.einsum("pms,mts->mpt", src_prb, blocks, precision=HIGH)
        is_live = jnp.arange(NEAR, dtype=jnp.int32) < near_count[leaf_id]
        return jnp.sum(jnp.where(is_live[:, None, None], contrib, jnp.zeros_like(contrib)), axis=0)

    near_part = lax.map(near_leaf, leaf_ids)

    def leaf_up(leaf_id):
        target = leaf_tiles[:, leaf_id]
        skel_pts = jnp.take(target, leaf_skel[leaf_id], axis=1)
        leaf_kernel = kernel_block(target, skel_pts)
        charge = jnp.dot(probe_tiles[:, leaf_id].astype(jnp.float32), leaf_kernel, precision=HIGH)
        return skel_pts, charge.astype(jnp.bfloat16)

    node_pts, node_q = lax.map(leaf_up, leaf_ids)
    sections = []
    local_rows = local_skel.reshape(N_LEAF, LEAF_DEV - 1, SKEL)
    for level_no in range(1, LOC_LEVELS + 1):
        offset = LEAF_DEV - (LEAF_DEV >> (level_no - 1))
        chosen = local_rows[:, offset:offset + (LEAF_DEV >> level_no)].reshape(-1, SKEL)
        node_pts, node_q, up_kernel, coupling = up_level(node_pts, node_q, chosen)
        sections.append((up_kernel, coupling))
    for bit_no in range(N_LEAF.bit_length() - 1):
        offset = N_LEAF - (N_LEAF >> bit_no)
        chosen = upper_skel[offset:offset + (N_LEAF >> (bit_no + 1))]
        node_pts, node_q, up_kernel, coupling = up_level(node_pts, node_q, chosen)
        sections.append((up_kernel, coupling))
    down_field = jnp.zeros((1, PROBES, SKEL), jnp.float32)
    for up_kernel, coupling in reversed(sections):
        down_field = descend(down_field, up_kernel, coupling)

    def leaf_down(inputs):
        leaf_id, field_row = inputs
        target = leaf_tiles[:, leaf_id]
        skel_pts = jnp.take(target, leaf_skel[leaf_id], axis=1)
        leaf_kernel = kernel_block(target, skel_pts)
        return jnp.dot(field_row, leaf_kernel.T, precision=HIGH)

    far_part = lax.map(leaf_down, (leaf_ids, down_field))
    response = near_part + far_part
    return jnp.transpose(response, (1, 0, 2)).reshape(PROBES, POINTS)
```

```python
import functools
import math

import jax
import jax.numpy as jnp
from jax import lax
from jax.experimental import pallas as pl
from jax.experimental.pallas import tpu as pltpu
from jax.sharding import PartitionSpec as P

F32 = jnp.float32
BF16 = jnp.bfloat16
AUG = 16
SQ_TOP = 3.0e38


def mm(a, b):
    return lax.dot_general(a, b, (((1,), (0,)), ((), ())), preferred_element_type=F32)


def mm_nt(a, b):
    return lax.dot_general(a, b, (((1,), (1,)), ((), ())), preferred_element_type=F32)


def mm_tn(a, b):
    return lax.dot_general(a, b, (((0,), (0,)), ((), ())), preferred_element_type=F32)


def halves(x):
    high = x.astype(BF16)
    return high, (x - high.astype(F32)).astype(BF16)


def square_rows(pts):
    wide = pts.astype(F32)
    sq = jnp.sum(wide * wide, axis=0, keepdims=True)
    neg = -0.5 * jnp.minimum(sq, SQ_TOP)
    one = neg.astype(BF16).astype(F32)
    rest = neg - one
    two = rest.astype(BF16).astype(F32)
    three = rest - two
    return one, two, three


def aug_rows(pieces, left, width):
    one, two, three = pieces
    row = lax.broadcasted_iota(jnp.int32, (AUG, width), 0)
    if not left:
        row = jnp.where(row < 3, row + 3, jnp.where(row < 6, row - 3, row))
    ones = jnp.where((row >= 3) & (row < 6), 1.0, 0.0)
    body = jnp.where(row == 0, one, jnp.where(row == 1, two, jnp.where(row == 2, three, ones)))
    return body.astype(BF16)


def affinity(left, right, emb):
    scale = 4.0 / emb * math.log2(math.e)
    return jnp.exp2(mm_tn(left, right) * scale)


def left_of(ext, emb):
    return ext[: emb + AUG]


def right_of(ext, emb):
    return jnp.concatenate([ext[:emb], ext[emb + AUG : emb + 2 * AUG]], axis=0)


def one_hot(chosen, pool):
    ids = lax.broadcasted_iota(jnp.int32, (pool, chosen.shape[1]), 0)
    return jnp.where(ids == chosen, 1.0, 0.0).astype(BF16)


def up_kernel(emb, leaf_num, leaf_len, pts_ref, prb_ref, leaf_skel_ref, local_skel_ref,
              root_ref, skel_ref, tree_ref, couple_ref, node_ref):
    skel_len = leaf_skel_ref.shape[1]
    ext_rows = emb + 2 * AUG

    def leaf_step(leaf, carry):
        cols = pl.ds(pl.multiple_of(leaf * leaf_len, leaf_len), leaf_len)
        pts = pts_ref[:, cols]
        pieces = square_rows(pts)
        left = jnp.concatenate([pts, aug_rows(pieces, True, leaf_len)], axis=0)
        ext = jnp.concatenate([left, aug_rows(pieces, False, leaf_len)], axis=0)
        hot = one_hot(leaf_skel_ref[pl.ds(leaf, 1), :], leaf_len)
        skel = mm(ext, hot).astype(BF16)
        kern = affinity(left, right_of(skel, emb), emb)
        high, low = halves(kern)
        prb = prb_ref[:, cols]
        node_ref[leaf, :ext_rows, :] = skel
        node_ref[leaf, ext_rows:, :] = (mm(prb, high) + mm(prb, low)).astype(BF16)
        skel_ref[leaf] = skel
        return carry

    lax.fori_loop(0, leaf_num, leaf_step, 0, unroll=2)

    start, row = 0, 0
    width = leaf_num // 2
    while width >= 1:
        def node_step(k, carry, start=start, row=row, width=width):
            child = start + 2 * k
            first = node_ref[child]
            second = node_ref[child + 1]
            first_ext, first_q = first[:ext_rows], first[ext_rows:]
            second_ext, second_q = second[:ext_rows], second[ext_rows:]
            joined = jnp.concatenate([first_ext, second_ext], axis=1)
            joined_q = jnp.concatenate([first_q, second_q], axis=1)
            hot = one_hot(local_skel_ref[pl.ds(row + k, 1), :], 2 * skel_len)
            parent = mm(joined, hot).astype(BF16)
            kern = affinity(left_of(joined, emb), right_of(parent, emb), emb)
            high, low = halves(kern)
            parent_q = (mm(joined_q, high) + mm(joined_q, low)).astype(BF16)
            tree_ref[row + k, : 2 * skel_len, :] = high
            tree_ref[row + k, 2 * skel_len :, :] = low
            target = start + 2 * width + k
            node_ref[target, :ext_rows, :] = parent
            node_ref[target, ext_rows:, :] = parent_q
            high, low = halves(affinity(left_of(second_ext, emb), right_of(first_ext, emb), emb))
            couple_ref[row + k, :, :skel_len] = mm(second_q, high) + mm(second_q, low)
            high, low = halves(affinity(left_of(first_ext, emb), right_of(second_ext, emb), emb))
            couple_ref[row + k, :, skel_len:] = mm(first_q, high) + mm(first_q, low)
            return carry

        lax.fori_loop(0, width, node_step, 0, unroll=min(width, 2))
        start, row, width = start + 2 * width, row + width, width // 2
    root_ref[...] = node_ref[start]


def level_kernel(emb, cur_ref, sib_ref, chosen_ref, next_ref, couple_ref, own_ref):
    skel_len = chosen_ref.shape[1]
    ext_rows = emb + 2 * AUG
    cur, sib = cur_ref[...], sib_ref[...]
    cur_ext, cur_q = cur[:ext_rows], cur[ext_rows:]
    sib_ext, sib_q = sib[:ext_rows], sib[ext_rows:]
    joined = jnp.concatenate([cur_ext, sib_ext], axis=1)
    joined_q = jnp.concatenate([cur_q, sib_q], axis=1)
    hot = one_hot(chosen_ref[...], 2 * skel_len)
    parent = mm(joined, hot).astype(BF16)
    kern = affinity(left_of(joined, emb), right_of(parent, emb), emb)
    high, low = halves(kern)
    next_ref[:ext_rows, :] = parent
    next_ref[ext_rows:, :] = (mm(joined_q, high) + mm(joined_q, low)).astype(BF16)
    own_ref[:skel_len, :] = high[:skel_len]
    own_ref[skel_len:, :] = low[:skel_len]
    high, low = halves(affinity(left_of(sib_ext, emb), right_of(cur_ext, emb), emb))
    couple_ref[...] = mm(sib_q, high) + mm(sib_q, low)


def near_kernel(emb, leaf_len, picks, tile, ids_ref, count_ref, pts_ref, *refs):
    num = len(picks)
    src_pts, src_prb = refs[:num], refs[num : 2 * num]
    base_ref = refs[2 * num] if len(refs) == 2 * num + 3 else None
    out_ref, right_ref = refs[-2:]
    leaf_num = count_ref.shape[0]

    def leaf_step(leaf, carry):
        cols = pl.ds(pl.multiple_of(leaf * leaf_len, leaf_len), leaf_len)
        target = pts_ref[:, cols]
        right_ref[:emb, :] = target
        right_ref[emb:, :] = aug_rows(square_rows(target), False, leaf_len)
        if base_ref is None:
            out_ref[:, cols] = jnp.zeros((out_ref.shape[0], leaf_len), F32)
        else:
            out_ref[:, cols] = base_ref[:, cols]

        def slot_step(slot, carry):
            source = ids_ref[leaf, slot]
            for k, (low, high) in enumerate(picks):
                @pl.when((source >= low) & (source < high))
                def _():
                    at = pl.ds(pl.multiple_of((source - low) * leaf_len, leaf_len), leaf_len)
                    pts = src_pts[k][:, at]
                    left = jnp.concatenate(
                        [pts, aug_rows(square_rows(pts), True, leaf_len)], axis=0)
                    prb = src_prb[k][:, at]
                    for c in range(0, leaf_len, tile):
                        right = right_ref[:, c : c + tile]
                        total = None
                        for s in range(0, leaf_len, tile):
                            kern = affinity(left[:, s : s + tile], right, emb).astype(BF16)
                            term = mm(prb[:, s : s + tile], kern)
                            total = term if total is None else total + term
                        at_c = pl.ds(pl.multiple_of(leaf * leaf_len + c, tile), tile)
                        out_ref[:, at_c] += total
            return carry

        lax.fori_loop(0, count_ref[leaf], slot_step, 0)
        return carry

    lax.fori_loop(0, leaf_num, leaf_step, 0)


def down_kernel(emb, leaf_num, leaf_len, level_num, *refs):
    owns, couples = refs[:level_num], refs[level_num : 2 * level_num]
    tree_ref, tree_couple_ref, skel_ref, pts_ref, near_ref, out_ref, field_ref = refs[2 * level_num :]
    skel_len = skel_ref.shape[2]
    probe_num = out_ref.shape[0]

    def spread(field, high, low):
        field_high, field_low = halves(field)
        both = mm_nt(jnp.concatenate([field_high, field_low], axis=0), high)
        return both[:probe_num] + both[probe_num:] + mm_nt(field_high, low)

    field = jnp.zeros((probe_num, skel_len), F32)
    for own, couple in zip(reversed(owns), reversed(couples)):
        field = spread(field, own[:skel_len], own[skel_len:]) + couple[...]

    node_total = 2 * leaf_num - 1
    field_ref[node_total - 1] = field
    width, row, start = 1, leaf_num - 2, node_total - 1
    while width < leaf_num:
        below = start - 2 * width

        def node_step(k, carry, row=row, start=start, below=below):
            both = spread(field_ref[start + k], tree_ref[row + k, : 2 * skel_len, :],
                          tree_ref[row + k, 2 * skel_len :, :]) + tree_couple_ref[row + k]
            field_ref[below + 2 * k] = both[:, :skel_len]
            field_ref[below + 2 * k + 1] = both[:, skel_len:]
            return carry

        lax.fori_loop(0, width, node_step, 0, unroll=min(width, 2))
        row, start, width = row - 2 * width, below, 2 * width

    def leaf_step(leaf, carry):
        cols = pl.ds(pl.multiple_of(leaf * leaf_len, leaf_len), leaf_len)
        pts = pts_ref[:, cols]
        right = jnp.concatenate([pts, aug_rows(square_rows(pts), False, leaf_len)], axis=0)
        high, low = halves(affinity(left_of(skel_ref[leaf], emb), right, emb))
        field_high, field_low = halves(field_ref[leaf])
        both = mm(jnp.concatenate([field_high, field_low], axis=0), high)
        far = both[:probe_num] + both[probe_num:] + mm(field_high, low)
        out_ref[:, cols] = near_ref[:, cols] + far
        return carry

    lax.fori_loop(0, leaf_num, leaf_step, 0, unroll=2)


def whole(num):
    return [pl.BlockSpec(memory_space=pltpu.VMEM)] * num


def params():
    return pltpu.CompilerParams(vmem_limit_bytes=48 * 1024 * 1024)


def cost(flops, read):
    return pl.CostEstimate(flops=flops, bytes_accessed=read, transcendentals=0)


def shift(block, axis, step):
    count = lax.axis_size(axis)
    if step > 0:
        return lax.ppermute(block, axis, [(i, i + 1) for i in range(count - 1)])
    return lax.ppermute(block, axis, [(i + 1, i) for i in range(count - 1)])


def partner(block, axis, stride):
    count = lax.axis_size(axis)
    return lax.ppermute(block, axis, [(i, i ^ (1 << stride)) for i in range(count)])


def per_device(points, probes, near_list, near_count, leaf_skel, local_skel, upper_skel):
    emb, shard_len = points.shape
    leaf_num, slot_num = near_list.shape
    leaf_len = shard_len // leaf_num
    skel_len = leaf_skel.shape[1]
    probe_num = probes.shape[0]
    me = lax.axis_index("leaf")
    dev_num = lax.axis_size("leaf")
    level_num = dev_num.bit_length() - 1
    node_rows = emb + 2 * AUG + probe_num
    node_total = 2 * leaf_num - 1

    before_pts, before_prb = shift(points, "leaf", 1), shift(probes, "leaf", 1)
    after_pts, after_prb = shift(points, "leaf", -1), shift(probes, "leaf", -1)

    local_ids = near_list - (me * leaf_num - leaf_num)
    bits = jnp.arange(level_num, dtype=jnp.int32)
    rows = dev_num - (dev_num >> bits) + (me >> (bits + 1))
    chosen = jnp.take(upper_skel, rows, axis=0) ^ (((me >> bits) & 1) * skel_len)[:, None]

    sd = jax.ShapeDtypeStruct
    cur, skel, tree, tree_couple = pl.pallas_call(
        functools.partial(up_kernel, emb, leaf_num, leaf_len),
        out_shape=(
            sd((node_rows, skel_len), BF16),
            sd((leaf_num, emb + 2 * AUG, skel_len), BF16),
            sd((leaf_num - 1, 4 * skel_len, skel_len), BF16),
            sd((leaf_num - 1, probe_num, 2 * skel_len), F32),
        ),
        in_specs=whole(4),
        out_specs=tuple(whole(4)),
        scratch_shapes=[pltpu.VMEM((node_total, node_rows, skel_len), BF16)],
        compiler_params=params(),
        cost_estimate=cost(5_000_000_000, 4_000_000),
        name="up",
    )(points, probes, leaf_skel, local_skel)

    smem = [pl.BlockSpec(memory_space=pltpu.SMEM)] * 2
    tile = min(256, leaf_len)
    near = pl.pallas_call(
        functools.partial(near_kernel, emb, leaf_len, ((leaf_num, 2 * leaf_num),), tile),
        out_shape=sd((probe_num, shard_len), F32),
        in_specs=smem + whole(3),
        out_specs=whole(1)[0],
        scratch_shapes=[pltpu.VMEM((emb + AUG, leaf_len), BF16)],
        compiler_params=params(),
        cost_estimate=cost(5_000_000_000, 4_000_000),
        name="near_own",
    )(local_ids, near_count, points, points, probes)

    owns, couples = [], []
    for level in range(level_num):
        sib = partner(cur, "leaf", level)
        cur, couple, own = pl.pallas_call(
            functools.partial(level_kernel, emb),
            out_shape=(
                sd((node_rows, skel_len), BF16),
                sd((probe_num, skel_len), F32),
                sd((2 * skel_len, skel_len), BF16),
            ),
            in_specs=whole(3),
            out_specs=tuple(whole(3)),
            compiler_params=params(),
            cost_estimate=cost(1_000_000_000, 200_000),
            name="level",
        )(cur, sib, chosen[level : level + 1])
        owns.append(own)
        couples.append(couple)

    near = pl.pallas_call(
        functools.partial(
            near_kernel, emb, leaf_len, ((0, leaf_num), (2 * leaf_num, 3 * leaf_num)), tile),
        out_shape=sd((probe_num, shard_len), F32),
        in_specs=smem + whole(6),
        out_specs=whole(1)[0],
        scratch_shapes=[pltpu.VMEM((emb + AUG, leaf_len), BF16)],
        compiler_params=params(),
        cost_estimate=cost(5_000_000_000, 4_000_000),
        name="near_beside",
    )(local_ids, near_count, points, before_pts, after_pts, before_prb, after_prb, near)

    return pl.pallas_call(
        functools.partial(down_kernel, emb, leaf_num, leaf_len, level_num),
        out_shape=sd((probe_num, shard_len), F32),
        in_specs=whole(2 * level_num + 5),
        out_specs=whole(1)[0],
        scratch_shapes=[pltpu.VMEM((node_total, probe_num, skel_len), F32)],
        compiler_params=params(),
        cost_estimate=cost(5_000_000_000, 4_000_000),
        name="down",
    )(*owns, *couples, tree, tree_couple, skel, points, near)


def solution(mesh):
    in_specs = (
        P(None, "leaf"),
        P(None, "leaf"),
        P("leaf", None),
        P("leaf"),
        P("leaf", None),
        P("leaf", None),
        P(),
    )
    return jax.shard_map(
        per_device, mesh=mesh, in_specs=in_specs, out_specs=P(None, "leaf"), check_vma=False
    )
```

```python
import functools
import math

import jax
import jax.numpy as jnp
from jax import lax
from jax.experimental import pallas as pl
from jax.experimental.pallas import tpu as pltpu
from jax.sharding import PartitionSpec as P

F32 = jnp.float32
BF16 = jnp.bfloat16
AUG = 16
SQ_TOP = 3.0e38
VMEM_MIB = 20
GROUP = 4
PIECE_LEVELS = (2, 4, 5, 7)


def mm(a, b):
    return lax.dot_general(a, b, (((1,), (0,)), ((), ())), preferred_element_type=F32)


def mm_nt(a, b):
    return lax.dot_general(a, b, (((1,), (1,)), ((), ())), preferred_element_type=F32)


def mm_tn(a, b):
    return lax.dot_general(a, b, (((0,), (0,)), ((), ())), preferred_element_type=F32)


def halves(x):
    high = x.astype(BF16)
    return high, (x - high.astype(F32)).astype(BF16)


def square_rows(pts):
    wide = pts.astype(F32)
    sq = jnp.sum(wide * wide, axis=0, keepdims=True)
    neg = -0.5 * jnp.minimum(sq, SQ_TOP)
    one = neg.astype(BF16).astype(F32)
    rest = neg - one
    two = rest.astype(BF16).astype(F32)
    three = rest - two
    return one, two, three


def aug_rows(pieces, left, width):
    one, two, three = pieces
    row = lax.broadcasted_iota(jnp.int32, (AUG, width), 0)
    if not left:
        row = jnp.where(row < 3, row + 3, jnp.where(row < 6, row - 3, row))
    ones = jnp.where((row >= 3) & (row < 6), 1.0, 0.0)
    body = jnp.where(row == 0, one, jnp.where(row == 1, two, jnp.where(row == 2, three, ones)))
    return body.astype(BF16)


def exp_scaled(z, emb):
    return jnp.exp2(z * (4.0 / emb * math.log2(math.e)))


def affinity(left, right, emb):
    return exp_scaled(mm_tn(left, right), emb)


def left_of(ext, emb):
    return ext[: emb + AUG]


def right_of(ext, emb):
    return jnp.concatenate([ext[:emb], ext[emb + AUG : emb + 2 * AUG]], axis=0)


def one_hot(chosen, pool):
    ids = lax.broadcasted_iota(jnp.int32, (pool, chosen.shape[1]), 0)
    return jnp.where(ids == chosen, 1.0, 0.0).astype(BF16)


def up_kernel(emb, leaf_num, leaf_len, group, pts_ref, prb_ref, leaf_skel_ref, local_skel_ref,
              root_ref, leaf_ref, tree_ref, couple_ref, left_ref, node_ref):
    skel_len = leaf_skel_ref.shape[1]
    ext_rows = emb + 2 * AUG

    def leaf_step(step, carry):
        ids = [step * group + k for k in range(group)]
        cols = [pl.ds(pl.multiple_of(leaf * leaf_len, leaf_len), leaf_len) for leaf in ids]
        hots = [one_hot(leaf_skel_ref[pl.ds(leaf, 1), :], leaf_len) for leaf in ids]
        exts = []
        for at in cols:
            pts = pts_ref[:, at]
            pieces = square_rows(pts)
            exts.append(jnp.concatenate(
                [pts, aug_rows(pieces, True, leaf_len), aug_rows(pieces, False, leaf_len)], axis=0))
        skels = [mm(ext, hot).astype(BF16) for ext, hot in zip(exts, hots)]
        zs = [mm_tn(left_of(skel, emb), right_of(ext, emb)) for skel, ext in zip(skels, exts)]
        lefts = [left_of(ext, emb).T for ext in exts]
        pairs = [halves(exp_scaled(z, emb)) for z in zs]
        charges = [
            (mm_nt(prb_ref[:, at], high) + mm_nt(prb_ref[:, at], low)).astype(BF16)
            for at, (high, low) in zip(cols, pairs)
        ]
        for leaf, left, skel, charge, (high, low) in zip(ids, lefts, skels, charges, pairs):
            left_ref[leaf] = left
            node_ref[leaf, :ext_rows, :] = skel
            node_ref[leaf, ext_rows:, :] = charge
            leaf_ref[leaf, :skel_len, :] = high
            leaf_ref[leaf, skel_len:, :] = low
        return carry

    lax.fori_loop(0, leaf_num // group, leaf_step, 0)

    start, row = 0, 0
    width = leaf_num // 2
    while width >= 1:
        part = min(width, group)
        for base in range(0, width, part):
            ks = range(base, base + part)
            hots = [one_hot(local_skel_ref[row + k : row + k + 1, :], 2 * skel_len) for k in ks]
            kids = [(node_ref[start + 2 * k], node_ref[start + 2 * k + 1]) for k in ks]
            exts = [(x[:ext_rows], y[:ext_rows]) for x, y in kids]
            qs = [(x[ext_rows:], y[ext_rows:]) for x, y in kids]
            joins = [jnp.concatenate(pair, axis=1) for pair in exts]
            parents = [mm(joined, hot).astype(BF16) for joined, hot in zip(joins, hots)]
            crosses = [mm_tn(left_of(x, emb), right_of(y, emb)) for x, y in exts]
            zs = [mm_tn(left_of(parent, emb), right_of(joined, emb))
                  for parent, joined in zip(parents, joins)]
            crosses = [halves(exp_scaled(z, emb)) for z in crosses]
            pairs = [halves(exp_scaled(z, emb)) for z in zs]
            parent_qs = []
            for (x, y), (high, low) in zip(qs, pairs):
                joined_q = jnp.concatenate([x, y], axis=1)
                parent_qs.append((mm_nt(joined_q, high) + mm_nt(joined_q, low)).astype(BF16))
            for k, (x, y), (high, low) in zip(ks, qs, crosses):
                couple_ref[row + k, :, :skel_len] = mm_nt(y, high) + mm_nt(y, low)
                couple_ref[row + k, :, skel_len:] = mm(x, high) + mm(x, low)
            for k, parent, parent_q, (high, low) in zip(ks, parents, parent_qs, pairs):
                tree_ref[row + k, :skel_len, :] = high
                tree_ref[row + k, skel_len:, :] = low
                target = start + 2 * width + k
                node_ref[target, :ext_rows, :] = parent
                node_ref[target, ext_rows:, :] = parent_q
        start, row, width = start + 2 * width, row + width, width // 2
    root_ref[...] = node_ref[start]


def level_kernel(emb, cur_ref, sib_ref, chosen_ref, next_ref, couple_ref, own_ref):
    skel_len = chosen_ref.shape[1]
    ext_rows = emb + 2 * AUG
    cur, sib = cur_ref[...], sib_ref[...]
    cur_ext, cur_q = cur[:ext_rows], cur[ext_rows:]
    sib_ext, sib_q = sib[:ext_rows], sib[ext_rows:]
    joined = jnp.concatenate([cur_ext, sib_ext], axis=1)
    joined_q = jnp.concatenate([cur_q, sib_q], axis=1)
    hot = one_hot(chosen_ref[...], 2 * skel_len)
    parent = mm(joined, hot).astype(BF16)
    high, low = halves(affinity(left_of(parent, emb), right_of(joined, emb), emb))
    next_ref[:ext_rows, :] = parent
    next_ref[ext_rows:, :] = (mm_nt(joined_q, high) + mm_nt(joined_q, low)).astype(BF16)
    own_ref[:skel_len, :] = high[:, :skel_len]
    own_ref[skel_len:, :] = low[:, :skel_len]
    high, low = halves(affinity(left_of(sib_ext, emb), right_of(cur_ext, emb), emb))
    couple_ref[...] = mm(sib_q, high) + mm(sib_q, low)


def near_kernel(emb, leaf_len, first, picks, batch, ids_ref, count_ref, left_ref, *refs):
    num = len(picks)
    src_pts, src_prb = refs[:num], refs[num : 2 * num]
    out_ref, acc_ref, list_ref = refs[2 * num :]
    leaf_num = out_ref.shape[1] // leaf_len
    half = min(256, leaf_len)
    acc_ref[...] = jnp.zeros_like(acc_ref)

    for k, (low, high) in enumerate(picks):
        def gather_leaf(leaf, filled):
            def gather_slot(slot, filled):
                source = ids_ref[first + leaf, slot]
                mine = (source >= low) & (source < high)
                list_ref[0, filled] = leaf
                list_ref[1, filled] = jnp.where(mine, source - low, 0)
                return filled + mine.astype(jnp.int32)

            return lax.fori_loop(0, count_ref[first + leaf], gather_slot, filled)

        filled = lax.fori_loop(0, leaf_num, gather_leaf, 0)
        for k2 in range(batch - 1):
            list_ref[0, filled + k2] = 0
            list_ref[1, filled + k2] = 0

        def step(at, carry):
            items = [at * batch + k2 for k2 in range(batch)]
            leaves = [list_ref[0, item] for item in items]
            rights, prbs = [], []
            for item in items:
                cols = pl.ds(pl.multiple_of(list_ref[1, item] * leaf_len, leaf_len), leaf_len)
                pts = src_pts[k][:, cols]
                rights.append(
                    jnp.concatenate([pts, aug_rows(square_rows(pts), False, leaf_len)], axis=0))
                prb = src_prb[k][:, cols]
                if batch > 1:
                    prb = jnp.where(item < filled, prb.astype(F32), 0.0).astype(BF16)
                prbs.append(prb)
            tiles = [(i, c) for i in range(batch) for c in range(0, leaf_len, half)]

            def product(i, c):
                return mm(left_ref[first + leaves[i], c : c + half, :], rights[i])

            terms, ahead, kern = {}, product(*tiles[0]), None
            for n, tile in enumerate(tiles):
                z = ahead
                if n + 1 < len(tiles):
                    ahead = product(*tiles[n + 1])
                last, kern = kern, exp_scaled(z, emb).astype(BF16)
                if n > 0:
                    terms[tiles[n - 1]] = mm_nt(prbs[tiles[n - 1][0]], last)
            terms[tiles[-1]] = mm_nt(prbs[-1], kern)
            for i, c in tiles:
                acc_ref[leaves[i], :, c : c + half] += terms[i, c]
            return carry

        lax.fori_loop(0, (filled + batch - 1) // batch, step, 0)

    for leaf in range(leaf_num):
        out_ref[:, leaf * leaf_len : (leaf + 1) * leaf_len] = acc_ref[leaf]


def down_kernel(leaf_num, leaf_len, level_num, piece_num, *refs):
    owns, couples = refs[:level_num], refs[level_num : 2 * level_num]
    tree_ref, tree_couple_ref, leaf_ref, own_near_ref = refs[2 * level_num : 2 * level_num + 4]
    pieces = refs[2 * level_num + 4 : 2 * level_num + 4 + piece_num]
    out_ref, field_ref = refs[-2:]
    skel_len = tree_ref.shape[1] // 2
    probe_num = out_ref.shape[0]

    def spread(field, high, low):
        field_high, field_low = halves(field)
        both = mm(jnp.concatenate([field_high, field_low], axis=0), high)
        return both[:probe_num] + both[probe_num:] + mm(field_high, low)

    field = jnp.zeros((probe_num, skel_len), F32)
    for own, couple in zip(reversed(owns), reversed(couples)):
        field = spread(field, own[:skel_len], own[skel_len:]) + couple[...]

    fields, row = [field], leaf_num - 2
    while len(fields) < leaf_num:
        below = []
        for k, field in enumerate(fields):
            both = spread(field, tree_ref[row + k, :skel_len, :],
                          tree_ref[row + k, skel_len:, :]) + tree_couple_ref[row + k]
            below += [both[:, :skel_len], both[:, skel_len:]]
        fields, row = below, row - len(below)
    for leaf, field in enumerate(fields):
        field_ref[leaf] = field

    piece_leaves = leaf_num // piece_num
    for leaf in range(leaf_num):
        far = spread(field_ref[leaf], leaf_ref[leaf, :skel_len, :], leaf_ref[leaf, skel_len:, :])
        cols = slice(leaf * leaf_len, (leaf + 1) * leaf_len)
        at = leaf % piece_leaves * leaf_len
        near = own_near_ref[:, cols] + pieces[leaf // piece_leaves][:, at : at + leaf_len]
        out_ref[:, cols] = near + far


def whole(num):
    return [pl.BlockSpec(memory_space=pltpu.VMEM)] * num


def params():
    return pltpu.CompilerParams(vmem_limit_bytes=VMEM_MIB * 1024 * 1024)


def cost(flops, read):
    return pl.CostEstimate(flops=flops, bytes_accessed=read, transcendentals=0)


def shift(block, axis, step):
    count = lax.axis_size(axis)
    if step > 0:
        return lax.ppermute(block, axis, [(i, i + 1) for i in range(count - 1)])
    return lax.ppermute(block, axis, [(i + 1, i) for i in range(count - 1)])


def partner(block, axis, stride):
    count = lax.axis_size(axis)
    return lax.ppermute(block, axis, [(i, i ^ (1 << stride)) for i in range(count)])


def per_device(points, probes, near_list, near_count, leaf_skel, local_skel, upper_skel):
    emb, shard_len = points.shape
    leaf_num, slot_num = near_list.shape
    leaf_len = shard_len // leaf_num
    skel_len = leaf_skel.shape[1]
    probe_num = probes.shape[0]
    me = lax.axis_index("leaf")
    dev_num = lax.axis_size("leaf")
    level_num = dev_num.bit_length() - 1
    node_rows = emb + 2 * AUG + probe_num
    node_total = 2 * leaf_num - 1

    before_pts, after_pts = shift(points, "leaf", 1), shift(points, "leaf", -1)

    local_ids = near_list - (me * leaf_num - leaf_num)
    bits = jnp.arange(level_num, dtype=jnp.int32)
    rows = dev_num - (dev_num >> bits) + (me >> (bits + 1))
    chosen = jnp.take(upper_skel, rows, axis=0) ^ (((me >> bits) & 1) * skel_len)[:, None]

    sd = jax.ShapeDtypeStruct
    cur, leaf_kern, tree, tree_couple, left = pl.pallas_call(
        functools.partial(up_kernel, emb, leaf_num, leaf_len, GROUP),
        out_shape=(
            sd((node_rows, skel_len), BF16),
            sd((leaf_num, 2 * skel_len, leaf_len), BF16),
            sd((leaf_num - 1, 2 * skel_len, 2 * skel_len), BF16),
            sd((leaf_num - 1, probe_num, 2 * skel_len), F32),
            sd((leaf_num, leaf_len, emb + AUG), BF16),
        ),
        in_specs=whole(4),
        out_specs=tuple(whole(5)),
        scratch_shapes=[pltpu.VMEM((node_total, node_rows, skel_len), BF16)],
        compiler_params=params(),
        cost_estimate=cost(5_000_000_000, 4_000_000),
        name="up",
    )(points, probes, leaf_skel, local_skel)

    def near_call(name, first, leaves, picks, sources, batch):
        smem = [pl.BlockSpec(memory_space=pltpu.SMEM)] * 2
        return pl.pallas_call(
            functools.partial(near_kernel, emb, leaf_len, first, picks, batch),
            out_shape=sd((probe_num, leaves * leaf_len), F32),
            in_specs=smem + whole(1 + len(sources)),
            out_specs=whole(1)[0],
            scratch_shapes=[
                pltpu.VMEM((leaves, probe_num, leaf_len), F32),
                pltpu.SMEM((2, leaves * slot_num + batch), jnp.int32),
            ],
            compiler_params=params(),
            cost_estimate=cost(leaves * 300_000_000, leaves * 250_000),
            name=name,
        )(local_ids, near_count, left, *sources)

    near = near_call("near_own", 0, leaf_num, ((leaf_num, 2 * leaf_num),), (points, probes), 2)
    cur, near, probes = lax.optimization_barrier((cur, near, probes))
    before_prb, after_prb = shift(probes, "leaf", 1), shift(probes, "leaf", -1)

    sides = ((0, leaf_num), (2 * leaf_num, 3 * leaf_num))
    beside = (before_pts, after_pts, before_prb, after_prb)
    owns, couples, pieces = [], [], []
    piece_leaves = leaf_num // len(PIECE_LEVELS)
    for level in range(level_num):
        sib = partner(cur, "leaf", level)
        if level in PIECE_LEVELS:
            cur, left = lax.optimization_barrier((cur, left))
            piece = near_call("near_beside", len(pieces) * piece_leaves, piece_leaves, sides, beside, 1)
            sib, piece = lax.optimization_barrier((sib, piece))
            pieces.append(piece)
        cur, couple, own = pl.pallas_call(
            functools.partial(level_kernel, emb),
            out_shape=(
                sd((node_rows, skel_len), BF16),
                sd((probe_num, skel_len), F32),
                sd((2 * skel_len, skel_len), BF16),
            ),
            in_specs=whole(3),
            out_specs=tuple(whole(3)),
            compiler_params=params(),
            cost_estimate=cost(1_000_000_000, 200_000),
            name="level",
        )(cur, sib, chosen[level : level + 1])
        owns.append(own)
        couples.append(couple)

    return pl.pallas_call(
        functools.partial(down_kernel, leaf_num, leaf_len, level_num, len(pieces)),
        out_shape=sd((probe_num, shard_len), F32),
        in_specs=whole(2 * level_num + 4 + len(pieces)),
        out_specs=whole(1)[0],
        scratch_shapes=[pltpu.VMEM((leaf_num, probe_num, skel_len), F32)],
        compiler_params=params(),
        cost_estimate=cost(5_000_000_000, 4_000_000),
        name="down",
    )(*owns, *couples, tree, tree_couple, leaf_kern, near, *pieces)


def solution(mesh):
    in_specs = (
        P(None, "leaf"),
        P(None, "leaf"),
        P("leaf", None),
        P("leaf"),
        P("leaf", None),
        P("leaf", None),
        P(),
    )
    return jax.shard_map(
        per_device, mesh=mesh, in_specs=in_specs, out_specs=P(None, "leaf"), check_vma=False
    )
```

```python
import functools
import math

import jax
import jax.numpy as jnp
from jax import lax
from jax.experimental import pallas as pl
from jax.experimental.pallas import tpu as pltpu
from jax.sharding import PartitionSpec as P

F32 = jnp.float32
BF16 = jnp.bfloat16
AUG = 16
SQ_TOP = 3.0e38
VMEM_MIB = 20
GROUP = 4
NEAR_TILE = 256
LINK_LEVELS = (1, 2)
CHIP_STARTS = (2, 3, 4, 5)
CHIP_LEVELS = (4, 5, 6, 7)


def mm(a, b):
    return lax.dot_general(a, b, (((1,), (0,)), ((), ())), preferred_element_type=F32)


def mm_nt(a, b):
    return lax.dot_general(a, b, (((1,), (1,)), ((), ())), preferred_element_type=F32)


def mm_tn(a, b):
    return lax.dot_general(a, b, (((0,), (0,)), ((), ())), preferred_element_type=F32)


def halves(x):
    high = x.astype(BF16)
    return high, (x - high.astype(F32)).astype(BF16)


def square_rows(pts):
    wide = pts.astype(F32)
    sq = jnp.sum(wide * wide, axis=0, keepdims=True)
    neg = -0.5 * jnp.minimum(sq, SQ_TOP)
    one = neg.astype(BF16).astype(F32)
    rest = neg - one
    two = rest.astype(BF16).astype(F32)
    three = rest - two
    return one, two, three


def aug_rows(pieces, left, width):
    one, two, three = pieces
    row = lax.broadcasted_iota(jnp.int32, (AUG, width), 0)
    if not left:
        row = jnp.where(row < 3, row + 3, jnp.where(row < 6, row - 3, row))
    ones = jnp.where((row >= 3) & (row < 6), 1.0, 0.0)
    body = jnp.where(row == 0, one, jnp.where(row == 1, two, jnp.where(row == 2, three, ones)))
    return body.astype(BF16)


def exp_scaled(z, emb):
    return jnp.exp2(z * (4.0 / emb * math.log2(math.e)))


def affinity(left, right, emb):
    return exp_scaled(mm_tn(left, right), emb)


def left_of(ext, emb):
    return ext[: emb + AUG]


def right_of(ext, emb):
    return jnp.concatenate([ext[:emb], ext[emb + AUG : emb + 2 * AUG]], axis=0)


def one_hot(chosen, pool):
    ids = lax.broadcasted_iota(jnp.int32, (pool, chosen.shape[1]), 0)
    return jnp.where(ids == chosen, 1.0, 0.0).astype(BF16)


def up_kernel(emb, leaf_num, leaf_len, group, all_ref, leaf_skel_ref, local_skel_ref,
              root_ref, leaf_ref, tree_ref, couple_ref, left_ref, node_ref):
    skel_len = leaf_skel_ref.shape[1]
    ext_rows = emb + 2 * AUG

    def leaf_step(step, carry):
        ids = [step * group + k for k in range(group)]
        cols = [pl.ds(pl.multiple_of(leaf * leaf_len, leaf_len), leaf_len) for leaf in ids]
        hots = [one_hot(leaf_skel_ref[pl.ds(leaf, 1), :], leaf_len) for leaf in ids]
        exts = []
        for at in cols:
            pts = all_ref[:emb, at]
            pieces = square_rows(pts)
            exts.append(jnp.concatenate(
                [pts, aug_rows(pieces, True, leaf_len), aug_rows(pieces, False, leaf_len)], axis=0))
        skels = [mm(ext, hot).astype(BF16) for ext, hot in zip(exts, hots)]
        zs = [mm_tn(left_of(skel, emb), right_of(ext, emb)) for skel, ext in zip(skels, exts)]
        lefts = [left_of(ext, emb).T for ext in exts]
        pairs = [halves(exp_scaled(z, emb)) for z in zs]
        charges = [
            (mm_nt(all_ref[emb:, at], high) + mm_nt(all_ref[emb:, at], low)).astype(BF16)
            for at, (high, low) in zip(cols, pairs)
        ]
        for leaf, left, skel, charge, (high, low) in zip(ids, lefts, skels, charges, pairs):
            left_ref[leaf] = left
            node_ref[leaf, :ext_rows, :] = skel
            node_ref[leaf, ext_rows:, :] = charge
            leaf_ref[leaf, :skel_len, :] = high
            leaf_ref[leaf, skel_len:, :] = low
        return carry

    lax.fori_loop(0, leaf_num // group, leaf_step, 0)

    start, row = 0, 0
    width = leaf_num // 2
    while width >= 1:
        part = min(width, group)
        for base in range(0, width, part):
            ks = range(base, base + part)
            hots = [one_hot(local_skel_ref[row + k : row + k + 1, :], 2 * skel_len) for k in ks]
            kids = [(node_ref[start + 2 * k], node_ref[start + 2 * k + 1]) for k in ks]
            exts = [(x[:ext_rows], y[:ext_rows]) for x, y in kids]
            qs = [(x[ext_rows:], y[ext_rows:]) for x, y in kids]
            joins = [jnp.concatenate(pair, axis=1) for pair in exts]
            parents = [mm(joined, hot).astype(BF16) for joined, hot in zip(joins, hots)]
            crosses = [mm_tn(left_of(x, emb), right_of(y, emb)) for x, y in exts]
            zs = [mm_tn(left_of(parent, emb), right_of(joined, emb))
                  for parent, joined in zip(parents, joins)]
            crosses = [halves(exp_scaled(z, emb)) for z in crosses]
            pairs = [halves(exp_scaled(z, emb)) for z in zs]
            parent_qs = []
            for (x, y), (high, low) in zip(qs, pairs):
                joined_q = jnp.concatenate([x, y], axis=1)
                parent_qs.append((mm_nt(joined_q, high) + mm_nt(joined_q, low)).astype(BF16))
            for k, (x, y), (high, low) in zip(ks, qs, crosses):
                couple_ref[row + k, :, :skel_len] = mm_nt(y, high) + mm_nt(y, low)
                couple_ref[row + k, :, skel_len:] = mm(x, high) + mm(x, low)
            for k, parent, parent_q, (high, low) in zip(ks, parents, parent_qs, pairs):
                tree_ref[row + k, :skel_len, :] = high
                tree_ref[row + k, skel_len:, :] = low
                target = start + 2 * width + k
                node_ref[target, :ext_rows, :] = parent
                node_ref[target, ext_rows:, :] = parent_q
        start, row, width = start + 2 * width, row + width, width // 2
    root_ref[...] = node_ref[start]


def level_kernel(emb, cur_ref, sib_ref, chosen_ref, next_ref, couple_ref, own_ref):
    skel_len = chosen_ref.shape[1]
    ext_rows = emb + 2 * AUG
    cur, sib = cur_ref[...], sib_ref[...]
    cur_ext, cur_q = cur[:ext_rows], cur[ext_rows:]
    sib_ext, sib_q = sib[:ext_rows], sib[ext_rows:]
    joined = jnp.concatenate([cur_ext, sib_ext], axis=1)
    joined_q = jnp.concatenate([cur_q, sib_q], axis=1)
    hot = one_hot(chosen_ref[...], 2 * skel_len)
    parent = mm(joined, hot).astype(BF16)
    high, low = halves(affinity(left_of(parent, emb), right_of(joined, emb), emb))
    next_ref[:ext_rows, :] = parent
    next_ref[ext_rows:, :] = (mm_nt(joined_q, high) + mm_nt(joined_q, low)).astype(BF16)
    own_ref[:skel_len, :] = high[:, :skel_len]
    own_ref[skel_len:, :] = low[:, :skel_len]
    high, low = halves(affinity(left_of(sib_ext, emb), right_of(cur_ext, emb), emb))
    couple_ref[...] = mm(sib_q, high) + mm(sib_q, low)


def near_sum(emb, leaf_len, bucket, lists_ref, fills_ref, left_ref, src_ref, out_ref):
    tile = min(NEAR_TILE, leaf_len)
    probe_num = out_ref.shape[0]

    def step(item, carry):
        leaf = lists_ref[2 * bucket, item]
        cols = pl.ds(pl.multiple_of(lists_ref[2 * bucket + 1, item] * leaf_len, leaf_len), leaf_len)
        pts = src_ref[:emb, cols]
        right = jnp.concatenate([pts, aug_rows(square_rows(pts), False, leaf_len)], axis=0)
        prb = src_ref[emb:, cols]
        starts = list(range(0, leaf_len, tile))
        terms, ahead, kern = [], mm(left_ref[leaf, :tile, :], right), None
        for n in range(len(starts)):
            z = ahead
            if n + 1 < len(starts):
                ahead = mm(left_ref[leaf, starts[n + 1] : starts[n + 1] + tile, :], right)
            last, kern = kern, exp_scaled(z, emb).astype(BF16)
            if n > 0:
                terms.append(mm_nt(prb, last))
        terms.append(mm_nt(prb, kern))
        at = pl.ds(pl.multiple_of(leaf * leaf_len, leaf_len), leaf_len)
        out_ref[:, at] += jnp.concatenate(terms, axis=1)
        return carry

    lax.fori_loop(0, fills_ref[bucket], step, 0)


def near_own_kernel(emb, leaf_len, link_span, chip_span, ids_ref, count_ref, left_ref, src_ref,
                    out_ref, lists_ref, fills_ref):
    leaf_num = count_ref.shape[0]
    link_parts = leaf_num // link_span
    out_ref[...] = jnp.zeros_like(out_ref)
    for bucket in range(fills_ref.shape[0]):
        fills_ref[bucket] = 0

    def scan_leaf(leaf, carry):
        def scan_slot(slot, carry):
            source = ids_ref[leaf, slot]
            on_link = source < leaf_num
            on_chip = source >= 2 * leaf_num
            rest = source - 2 * leaf_num
            part = lax.div(jnp.maximum(rest, 0), chip_span)
            bucket = jnp.where(
                on_link, 1 + lax.div(source, link_span),
                jnp.where(on_chip, 1 + link_parts + part, 0))
            place = jnp.where(
                on_link, source,
                jnp.where(on_chip, rest - part * chip_span, source - leaf_num))
            filled = fills_ref[bucket]
            lists_ref[2 * bucket, filled] = leaf
            lists_ref[2 * bucket + 1, filled] = place
            fills_ref[bucket] = filled + 1
            return carry

        return lax.fori_loop(0, count_ref[leaf], scan_slot, carry)

    lax.fori_loop(0, leaf_num, scan_leaf, 0)
    near_sum(emb, leaf_len, 0, lists_ref, fills_ref, left_ref, src_ref, out_ref)


def near_kernel(emb, leaf_len, buckets, lists_ref, fills_ref, left_ref, *refs):
    base_ref, out_ref = refs[-2:]
    for bucket, src_ref in zip(buckets, refs[:-2]):
        near_sum(emb, leaf_len, bucket, lists_ref, fills_ref, left_ref, src_ref, out_ref)


def down_kernel(leaf_num, leaf_len, level_num, *refs):
    owns, couples = refs[:level_num], refs[level_num : 2 * level_num]
    tree_ref, tree_couple_ref, leaf_ref, near_ref, out_ref, field_ref = refs[2 * level_num :]
    skel_len = tree_ref.shape[1] // 2
    probe_num = out_ref.shape[0]

    def spread(field, high, low):
        field_high, field_low = halves(field)
        both = mm(jnp.concatenate([field_high, field_low], axis=0), high)
        return both[:probe_num] + both[probe_num:] + mm(field_high, low)

    field = jnp.zeros((probe_num, skel_len), F32)
    for own, couple in zip(reversed(owns), reversed(couples)):
        field = spread(field, own[:skel_len], own[skel_len:]) + couple[...]

    fields, row = [field], leaf_num - 2
    while len(fields) < leaf_num:
        below = []
        for k, field in enumerate(fields):
            both = spread(field, tree_ref[row + k, :skel_len, :],
                          tree_ref[row + k, skel_len:, :]) + tree_couple_ref[row + k]
            below += [both[:, :skel_len], both[:, skel_len:]]
        fields, row = below, row - len(below)
    for leaf, field in enumerate(fields):
        field_ref[leaf] = field

    for leaf in range(leaf_num):
        far = spread(field_ref[leaf], leaf_ref[leaf, :skel_len, :], leaf_ref[leaf, skel_len:, :])
        cols = slice(leaf * leaf_len, (leaf + 1) * leaf_len)
        out_ref[:, cols] = near_ref[:, cols] + far


def whole(num):
    return [pl.BlockSpec(memory_space=pltpu.VMEM)] * num


def params():
    return pltpu.CompilerParams(vmem_limit_bytes=VMEM_MIB * 1024 * 1024)


def cost(flops, read):
    return pl.CostEstimate(flops=flops, bytes_accessed=read, transcendentals=0)


def across_link(block, axis):
    count = lax.axis_size(axis)
    route = [(i, i + 1) for i in range(1, count - 1, 2)]
    return lax.ppermute(block, axis, route + [(j, i) for i, j in route])


def partner(block, axis, stride):
    count = lax.axis_size(axis)
    return lax.ppermute(block, axis, [(i, i ^ (1 << stride)) for i in range(count)])


def per_device(points, probes, near_list, near_count, leaf_skel, local_skel, upper_skel):
    emb, shard_len = points.shape
    leaf_num, slot_num = near_list.shape
    leaf_len = shard_len // leaf_num
    skel_len = leaf_skel.shape[1]
    probe_num = probes.shape[0]
    me = lax.axis_index("leaf")
    dev_num = lax.axis_size("leaf")
    level_num = dev_num.bit_length() - 1
    node_rows = emb + 2 * AUG + probe_num
    node_total = 2 * leaf_num - 1

    joined = jnp.concatenate([points, probes], axis=0)
    link = across_link(joined, "leaf")

    relative = near_list - (me * leaf_num - leaf_num)
    odd = (me & 1) == 1
    relative = jnp.where(
        odd & (relative < leaf_num), relative + 2 * leaf_num,
        jnp.where(odd & (relative >= 2 * leaf_num), relative - 2 * leaf_num, relative))
    bits = jnp.arange(level_num, dtype=jnp.int32)
    rows = dev_num - (dev_num >> bits) + (me >> (bits + 1))
    chosen = jnp.take(upper_skel, rows, axis=0) ^ (((me >> bits) & 1) * skel_len)[:, None]

    sd = jax.ShapeDtypeStruct
    cur, leaf_kern, tree, tree_couple, left = pl.pallas_call(
        functools.partial(up_kernel, emb, leaf_num, leaf_len, GROUP),
        out_shape=(
            sd((node_rows, skel_len), BF16),
            sd((leaf_num, 2 * skel_len, leaf_len), BF16),
            sd((leaf_num - 1, 2 * skel_len, 2 * skel_len), BF16),
            sd((leaf_num - 1, probe_num, 2 * skel_len), F32),
            sd((leaf_num, leaf_len, emb + AUG), BF16),
        ),
        in_specs=whole(3),
        out_specs=tuple(whole(5)),
        scratch_shapes=[pltpu.VMEM((node_total, node_rows, skel_len), BF16)],
        compiler_params=params(),
        cost_estimate=cost(5_000_000_000, 4_000_000),
        name="up",
    )(joined, leaf_skel, local_skel)

    link_parts, chip_parts = len(LINK_LEVELS), len(CHIP_LEVELS)
    link_span, chip_span = leaf_num // link_parts, leaf_num // chip_parts
    bucket_num = 1 + link_parts + chip_parts
    smem = [pl.BlockSpec(memory_space=pltpu.SMEM)] * 2
    near, lists, fills = pl.pallas_call(
        functools.partial(near_own_kernel, emb, leaf_len, link_span, chip_span),
        out_shape=(
            sd((probe_num, shard_len), F32),
            sd((2 * bucket_num, leaf_num * slot_num), jnp.int32),
            sd((bucket_num,), jnp.int32),
        ),
        in_specs=smem + whole(2),
        out_specs=tuple(whole(1) + smem),
        compiler_params=params(),
        cost_estimate=cost(5_000_000_000, 4_000_000),
        name="near_own",
    )(relative, near_count, left, joined)

    def near_call(near, buckets, sources):
        return pl.pallas_call(
            functools.partial(near_kernel, emb, leaf_len, buckets),
            out_shape=sd(near.shape, F32),
            in_specs=smem + whole(2 + len(sources)),
            out_specs=whole(1)[0],
            input_output_aliases={3 + len(sources): 0},
            compiler_params=params(),
            cost_estimate=cost(1_000_000_000, 1_000_000),
            name="near_beside",
        )(lists, fills, left, *sources, near)

    chunk = chip_span * leaf_len
    chunks = [joined[:, k * chunk : (k + 1) * chunk] for k in range(chip_parts)]
    cur, near, chosen, chunks = lax.optimization_barrier((cur, near, chosen, chunks))

    owns, couples = [], []
    for level in range(level_num):
        sib = partner(cur, "leaf", level)
        if level in CHIP_STARTS:
            k = CHIP_STARTS.index(level)
            chunks[k], cur = lax.optimization_barrier((chunks[k], cur))
            chunks[k] = partner(chunks[k], "leaf", 0)
        buckets, sources = [], []
        if level in LINK_LEVELS:
            buckets.append(1 + LINK_LEVELS.index(level))
            sources.append(link)
        if level in CHIP_LEVELS:
            k = CHIP_LEVELS.index(level)
            buckets.append(1 + link_parts + k)
            sources.append(chunks[k])
        if buckets:
            cur, near = lax.optimization_barrier((cur, near))
            near = near_call(near, tuple(buckets), sources)
            sib, near = lax.optimization_barrier((sib, near))
        cur, couple, own = pl.pallas_call(
            functools.partial(level_kernel, emb),
            out_shape=(
                sd((node_rows, skel_len), BF16),
                sd((probe_num, skel_len), F32),
                sd((2 * skel_len, skel_len), BF16),
            ),
            in_specs=whole(3),
            out_specs=tuple(whole(3)),
            compiler_params=params(),
            cost_estimate=cost(1_000_000_000, 200_000),
            name="level",
        )(cur, sib, chosen[level : level + 1])
        owns.append(own)
        couples.append(couple)

    return pl.pallas_call(
        functools.partial(down_kernel, leaf_num, leaf_len, level_num),
        out_shape=sd((probe_num, shard_len), F32),
        in_specs=whole(2 * level_num + 4),
        out_specs=whole(1)[0],
        scratch_shapes=[pltpu.VMEM((leaf_num, probe_num, skel_len), F32)],
        compiler_params=params(),
        cost_estimate=cost(5_000_000_000, 4_000_000),
        name="down",
    )(*owns, *couples, tree, tree_couple, leaf_kern, near)


def solution(mesh):
    in_specs = (
        P(None, "leaf"),
        P(None, "leaf"),
        P("leaf", None),
        P("leaf"),
        P("leaf", None),
        P("leaf", None),
        P(),
    )
    return jax.shard_map(
        per_device, mesh=mesh, in_specs=in_specs, out_specs=P(None, "leaf"), check_vma=False
    )
```

```python
import functools
import math

import jax
import jax.numpy as jnp
from jax import lax
from jax.experimental import pallas as pl
from jax.experimental.pallas import tpu as pltpu
from jax.sharding import PartitionSpec as P


F32 = jnp.float32
BF16 = jnp.bfloat16
AUG = 16
SQ_TOP = 3.0e38
VMEM_MIB = 20
GROUP = 8
NEAR_TILE = 512
CHIP_PARTS = 4
SENDS = {2: (0,), 3: (1,), 4: (2,), 5: (3,)}
SUMS = {
    2: (2, (-1,)),
    3: (3, (-1,)),
    4: (4, (-1, 0)),
    5: (12, (-1, 0, 1)),
    6: (4, (-1, 0, 1, 2)),
    7: (None, (-1, 0, 1, 2, 3)),
}


def mm(a, b):
    return lax.dot_general(a, b, (((1,), (0,)), ((), ())), preferred_element_type=F32)


def mm_nt(a, b):
    return lax.dot_general(a, b, (((1,), (1,)), ((), ())), preferred_element_type=F32)


def mm_tn(a, b):
    return lax.dot_general(a, b, (((0,), (0,)), ((), ())), preferred_element_type=F32)


def halves(x):
    high = x.astype(BF16)
    return high, (x - high.astype(F32)).astype(BF16)


def square_rows(pts):
    wide = pts.astype(F32)
    sq = jnp.sum(wide * wide, axis=0, keepdims=True)
    neg = -0.5 * jnp.minimum(sq, SQ_TOP)
    one = neg.astype(BF16).astype(F32)
    rest = neg - one
    two = rest.astype(BF16).astype(F32)
    three = rest - two
    return one, two, three


def aug_rows(pieces, left, width):
    one, two, three = pieces
    row = lax.broadcasted_iota(jnp.int32, (AUG, width), 0)
    if not left:
        row = jnp.where(row < 3, row + 3, jnp.where(row < 6, row - 3, row))
    ones = jnp.where((row >= 3) & (row < 6), 1.0, 0.0)
    body = jnp.where(row == 0, one, jnp.where(row == 1, two, jnp.where(row == 2, three, ones)))
    return body.astype(BF16)


def exp_scaled(z, emb):
    return jnp.exp2(z * (4.0 / emb * math.log2(math.e)))


def affinity(left, right, emb):
    return exp_scaled(mm_tn(left, right), emb)


def left_of(ext, emb):
    return ext[: emb + AUG]


def right_of(ext, emb):
    return jnp.concatenate([ext[:emb], ext[emb + AUG : emb + 2 * AUG]], axis=0)


def one_hot(chosen, pool):
    ids = lax.broadcasted_iota(jnp.int32, (pool, chosen.shape[1]), 0)
    return jnp.where(ids == chosen, 1.0, 0.0).astype(BF16)


def up_kernel(emb, leaf_num, leaf_len, group, all_ref, leaf_skel_ref, local_skel_ref,
              root_ref, leaf_ref, tree_ref, couple_ref, left_ref, node_ref):
    skel_len = leaf_skel_ref.shape[1]
    ext_rows = emb + 2 * AUG

    def leaf_step(step, carry):
        ids = [step * group + k for k in range(group)]
        cols = [pl.ds(pl.multiple_of(leaf * leaf_len, leaf_len), leaf_len) for leaf in ids]
        hots = [one_hot(leaf_skel_ref[pl.ds(leaf, 1), :], leaf_len) for leaf in ids]
        exts = []
        for at in cols:
            pts = all_ref[:emb, at]
            pieces = square_rows(pts)
            exts.append(jnp.concatenate(
                [pts, aug_rows(pieces, True, leaf_len), aug_rows(pieces, False, leaf_len)], axis=0))
        skels = [mm(ext, hot).astype(BF16) for ext, hot in zip(exts, hots)]
        zs = [mm_tn(left_of(skel, emb), right_of(ext, emb)) for skel, ext in zip(skels, exts)]
        lefts = [left_of(ext, emb).T for ext in exts]
        pairs = [halves(exp_scaled(z, emb)) for z in zs]
        charges = [
            (mm_nt(all_ref[emb:, at], high) + mm_nt(all_ref[emb:, at], low)).astype(BF16)
            for at, (high, low) in zip(cols, pairs)
        ]
        for leaf, left, skel, charge, (high, low) in zip(ids, lefts, skels, charges, pairs):
            left_ref[leaf] = left
            node_ref[leaf, :ext_rows, :] = skel
            node_ref[leaf, ext_rows:, :] = charge
            leaf_ref[leaf, :skel_len, :] = high
            leaf_ref[leaf, skel_len:, :] = low
        return carry

    lax.fori_loop(0, leaf_num // group, leaf_step, 0)

    start, row = 0, 0
    width = leaf_num // 2
    while width >= 1:
        part = min(width, group)
        for base in range(0, width, part):
            ks = range(base, base + part)
            hots = [one_hot(local_skel_ref[row + k : row + k + 1, :], 2 * skel_len) for k in ks]
            kids = [(node_ref[start + 2 * k], node_ref[start + 2 * k + 1]) for k in ks]
            exts = [(x[:ext_rows], y[:ext_rows]) for x, y in kids]
            qs = [(x[ext_rows:], y[ext_rows:]) for x, y in kids]
            joins = [jnp.concatenate(pair, axis=1) for pair in exts]
            parents = [mm(joined, hot).astype(BF16) for joined, hot in zip(joins, hots)]
            crosses = [mm_tn(left_of(x, emb), right_of(y, emb)) for x, y in exts]
            zs = [mm_tn(left_of(parent, emb), right_of(joined, emb))
                  for parent, joined in zip(parents, joins)]
            crosses = [halves(exp_scaled(z, emb)) for z in crosses]
            pairs = [halves(exp_scaled(z, emb)) for z in zs]
            parent_qs = []
            for (x, y), (high, low) in zip(qs, pairs):
                joined_q = jnp.concatenate([x, y], axis=1)
                parent_qs.append((mm_nt(joined_q, high) + mm_nt(joined_q, low)).astype(BF16))
            for k, (x, y), (high, low) in zip(ks, qs, crosses):
                couple_ref[row + k, :, :skel_len] = mm_nt(y, high) + mm_nt(y, low)
                couple_ref[row + k, :, skel_len:] = mm(x, high) + mm(x, low)
            for k, parent, parent_q, (high, low) in zip(ks, parents, parent_qs, pairs):
                tree_ref[row + k, :skel_len, :] = high
                tree_ref[row + k, skel_len:, :] = low
                target = start + 2 * width + k
                node_ref[target, :ext_rows, :] = parent
                node_ref[target, ext_rows:, :] = parent_q
        start, row, width = start + 2 * width, row + width, width // 2
    root_ref[...] = node_ref[start]


def level_kernel(emb, cur_ref, sib_ref, chosen_ref, couple_ref, own_ref, next_ref=None):
    skel_len = chosen_ref.shape[1]
    ext_rows = emb + 2 * AUG
    cur, sib = cur_ref[...], sib_ref[...]
    cur_ext, cur_q = cur[:ext_rows], cur[ext_rows:]
    sib_ext, sib_q = sib[:ext_rows], sib[ext_rows:]
    joined = jnp.concatenate([cur_ext, sib_ext], axis=1)
    joined_q = jnp.concatenate([cur_q, sib_q], axis=1)
    hot = one_hot(chosen_ref[...], 2 * skel_len)
    parent = mm(joined, hot).astype(BF16)
    high, low = halves(affinity(left_of(parent, emb), right_of(joined, emb), emb))
    if next_ref is not None:
        next_ref[:ext_rows, :] = parent
        next_ref[ext_rows:, :] = (mm_nt(joined_q, high) + mm_nt(joined_q, low)).astype(BF16)
    own_ref[:skel_len, :] = high[:, :skel_len]
    own_ref[skel_len:, :] = low[:, :skel_len]
    high, low = halves(affinity(left_of(sib_ext, emb), right_of(cur_ext, emb), emb))
    couple_ref[...] = mm(sib_q, high) + mm(sib_q, low)


def near_sum(leaf_len, bucket, first, last, lists_ref, left_ref, pts_ref, prb_ref, out_ref):
    tile = min(NEAR_TILE, leaf_len)
    emb = pts_ref.shape[0]

    def step(item, carry):
        leaf = lists_ref[2 * bucket, item]
        place = lists_ref[2 * bucket + 1, item]
        cols = pl.ds(pl.multiple_of(place * leaf_len, leaf_len), leaf_len)
        pts = pts_ref[:, cols]
        right = jnp.concatenate([pts, aug_rows(square_rows(pts), False, leaf_len)], axis=0)
        prb = prb_ref[:, cols]
        starts = list(range(0, leaf_len, tile))
        terms, ahead, kern = [], mm(left_ref[leaf, :tile, :], right), None
        for n in range(len(starts)):
            z = ahead
            if n + 1 < len(starts):
                ahead = mm(left_ref[leaf, starts[n + 1] : starts[n + 1] + tile, :], right)
            last, kern = kern, exp_scaled(z, emb).astype(BF16)
            if n > 0:
                terms.append(mm_nt(prb, last))
        terms.append(mm_nt(prb, kern))
        at = pl.ds(pl.multiple_of(leaf * leaf_len, leaf_len), leaf_len)
        out_ref[:, at] += jnp.concatenate(terms, axis=1)
        return carry

    lax.fori_loop(first, last, step, 0)


def near_own_kernel(emb, leaf_len, chip_span, ids_ref, count_ref, left_ref, all_ref,
                    out_ref, lists_ref):
    leaf_num = count_ref.shape[0]
    bucket_num = lists_ref.shape[0] // 2
    unused, lengths = bucket_num - 1, 2 * bucket_num
    out_ref[...] = jnp.zeros_like(out_ref)
    for bucket in range(bucket_num):
        lists_ref[lengths, bucket] = 0

    def scan_leaf(leaf, carry):
        count = count_ref[leaf]
        for slot in range(ids_ref.shape[1]):
            source = ids_ref[leaf, slot]
            on_link = source < leaf_num
            on_chip = source >= 2 * leaf_num
            home = source - jnp.where(on_link, 0, jnp.where(on_chip, 2 * leaf_num, leaf_num))
            part = jnp.where(on_chip, lax.div(home, chip_span), 0)
            bucket = jnp.where(on_link, 1, jnp.where(on_chip, 2 + part, 0))
            bucket = jnp.where(slot < count, bucket, unused)
            filled = lists_ref[lengths, bucket]
            lists_ref[2 * bucket, filled] = leaf
            lists_ref[2 * bucket + 1, filled] = home - part * chip_span
            lists_ref[lengths, bucket] = filled + 1
        return carry

    lax.fori_loop(0, leaf_num, scan_leaf, 0, unroll=4)
    near_sum(leaf_len, 0, 0, lists_ref[lengths, 0], lists_ref, left_ref,
             all_ref.at[:emb], all_ref.at[emb:], out_ref)


def near_kernel(emb, leaf_len, turns, lists_ref, left_ref, *refs):
    _, out_ref = refs[-2:]
    lengths = lists_ref.shape[0] - 1
    done = {}
    for turn, (budget, buckets) in enumerate(turns):
        for bucket, src_ref in zip(buckets, refs[:-2]):
            first = done.get(bucket, 0)
            count = lists_ref[lengths, bucket] - first
            if budget is not None:
                count = jnp.minimum(count, budget)
                budget = budget - count
            done[bucket] = first + count
            if turn + 1 == len(turns):
                near_sum(leaf_len, bucket, first, first + count, lists_ref, left_ref,
                         src_ref.at[:emb], src_ref.at[emb:], out_ref)


def down_kernel(leaf_num, leaf_len, level_num, *refs):
    owns, couples = refs[:level_num], refs[level_num : 2 * level_num]
    tree_ref, tree_couple_ref, leaf_ref, near_ref, out_ref, field_ref = refs[2 * level_num :]
    skel_len = tree_ref.shape[1] // 2
    probe_num = out_ref.shape[0]

    def spread(field, high, low):
        field_high, field_low = halves(field)
        both = mm(jnp.concatenate([field_high, field_low], axis=0), high)
        return both[:probe_num] + both[probe_num:] + mm(field_high, low)

    field = jnp.zeros((probe_num, skel_len), F32)
    for own, couple in zip(reversed(owns), reversed(couples)):
        field = spread(field, own[:skel_len], own[skel_len:]) + couple[...]

    fields, row = [field], leaf_num - 2
    while len(fields) < leaf_num:
        below = []
        for k, field in enumerate(fields):
            both = spread(field, tree_ref[row + k, :skel_len, :],
                          tree_ref[row + k, skel_len:, :]) + tree_couple_ref[row + k]
            below += [both[:, :skel_len], both[:, skel_len:]]
        fields, row = below, row - len(below)
    for leaf, field in enumerate(fields):
        field_ref[leaf] = field

    for leaf in range(leaf_num):
        far = spread(field_ref[leaf], leaf_ref[leaf, :skel_len, :], leaf_ref[leaf, skel_len:, :])
        cols = slice(leaf * leaf_len, (leaf + 1) * leaf_len)
        out_ref[:, cols] = near_ref[:, cols] + far


def whole(num):
    return [pl.BlockSpec(memory_space=pltpu.VMEM)] * num


def params():
    return pltpu.CompilerParams(vmem_limit_bytes=VMEM_MIB * 1024 * 1024)


def cost(flops, read):
    return pl.CostEstimate(flops=flops, bytes_accessed=read, transcendentals=0)


def across_link(block, axis):
    count = lax.axis_size(axis)
    route = [(i, i + 1) for i in range(1, count - 1, 2)]
    return lax.ppermute(block, axis, route + [(j, i) for i, j in route])


def partner(block, axis, stride):
    count = lax.axis_size(axis)
    return lax.ppermute(block, axis, [(i, i ^ (1 << stride)) for i in range(count)])


def per_device(points, probes, near_list, near_count, leaf_skel, local_skel, upper_skel):
    emb, shard_len = points.shape
    leaf_num, slot_num = near_list.shape
    leaf_len = shard_len // leaf_num
    skel_len = leaf_skel.shape[1]
    probe_num = probes.shape[0]
    me = lax.axis_index("leaf")
    dev_num = lax.axis_size("leaf")
    level_num = dev_num.bit_length() - 1
    node_rows = emb + 2 * AUG + probe_num
    node_total = 2 * leaf_num - 1

    chip_span = leaf_num // CHIP_PARTS

    joined = jnp.concatenate([points, probes], axis=0)
    link = across_link(joined, "leaf")

    relative = near_list - (me * leaf_num - leaf_num)
    odd = (me & 1) == 1
    relative = jnp.where(
        odd & (relative < leaf_num), relative + 2 * leaf_num,
        jnp.where(odd & (relative >= 2 * leaf_num), relative - 2 * leaf_num, relative))
    bits = jnp.arange(level_num, dtype=jnp.int32)
    rows = dev_num - (dev_num >> bits) + (me >> (bits + 1))
    chosen = jnp.take(upper_skel, rows, axis=0) ^ (((me >> bits) & 1) * skel_len)[:, None]

    sd = jax.ShapeDtypeStruct
    cur, leaf_kern, tree, tree_couple, left = pl.pallas_call(
        functools.partial(up_kernel, emb, leaf_num, leaf_len, GROUP),
        out_shape=(
            sd((node_rows, skel_len), BF16),
            sd((leaf_num, 2 * skel_len, leaf_len), BF16),
            sd((leaf_num - 1, 2 * skel_len, 2 * skel_len), BF16),
            sd((leaf_num - 1, probe_num, 2 * skel_len), F32),
            sd((leaf_num, leaf_len, emb + AUG), BF16),
        ),
        in_specs=whole(3),
        out_specs=tuple(whole(5)),
        scratch_shapes=[pltpu.VMEM((node_total, node_rows, skel_len), BF16)],
        compiler_params=params(),
        cost_estimate=cost(5_000_000_000, 4_000_000),
        name="up",
    )(joined, leaf_skel, local_skel)

    bucket_num = 3 + CHIP_PARTS
    smem = [pl.BlockSpec(memory_space=pltpu.SMEM)]
    near, lists = pl.pallas_call(
        functools.partial(near_own_kernel, emb, leaf_len, chip_span),
        out_shape=(
            sd((probe_num, shard_len), F32),
            sd((2 * bucket_num + 1, leaf_num * slot_num), jnp.int32),
        ),
        in_specs=smem * 2 + whole(2),
        out_specs=tuple(whole(1) + smem),
        compiler_params=params(),
        cost_estimate=cost(5_000_000_000, 4_000_000),
        name="near_own",
    )(relative, near_count, left, joined)

    def near_call(near, turns, sources):
        return pl.pallas_call(
            functools.partial(near_kernel, emb, leaf_len, turns),
            out_shape=sd(near.shape, F32),
            in_specs=smem + whole(2 + len(sources)),
            out_specs=whole(1)[0],
            input_output_aliases={2 + len(sources): 0},
            compiler_params=params(),
            cost_estimate=cost(1_000_000_000, 1_000_000),
            name="near_beside",
        )(lists, left, *sources, near)

    chip_wide = chip_span * leaf_len
    parts = [joined[:, k * chip_wide : (k + 1) * chip_wide] for k in range(CHIP_PARTS)]
    cur, near, chosen, parts = lax.optimization_barrier((cur, near, chosen, parts))
    arrived, turns = {-1: link}, ()

    owns, couples = [], []
    for level in range(level_num):
        sib = partner(cur, "leaf", level)
        for k in SENDS.get(level, ()):
            part, cur = lax.optimization_barrier((parts[k], cur))
            arrived[k] = partner(part, "leaf", 0)
        if level in SUMS:
            budget, ks = SUMS[level]
            turns += ((budget, tuple(2 + k for k in ks)),)
            cur, near = lax.optimization_barrier((cur, near))
            near = near_call(near, turns, [arrived[k] for k in ks])
            sib, near = lax.optimization_barrier((sib, near))
        more = 1 if level + 1 < level_num else 0
        couple, own, *rest = pl.pallas_call(
            functools.partial(level_kernel, emb),
            out_shape=(
                sd((probe_num, skel_len), F32),
                sd((2 * skel_len, skel_len), BF16),
            ) + (sd((node_rows, skel_len), BF16),) * more,
            in_specs=whole(3),
            out_specs=tuple(whole(2 + more)),
            compiler_params=params(),
            cost_estimate=cost(1_000_000_000, 200_000),
            name="level",
        )(cur, sib, chosen[level : level + 1])
        if rest:
            cur = rest[0]
        owns.append(own)
        couples.append(couple)

    return pl.pallas_call(
        functools.partial(down_kernel, leaf_num, leaf_len, level_num),
        out_shape=sd((probe_num, shard_len), F32),
        in_specs=whole(2 * level_num + 4),
        out_specs=whole(1)[0],
        scratch_shapes=[pltpu.VMEM((leaf_num, probe_num, skel_len), F32)],
        compiler_params=params(),
        cost_estimate=cost(5_000_000_000, 4_000_000),
        name="down",
    )(*owns, *couples, tree, tree_couple, leaf_kern, near)


def solution(mesh):
    in_specs = (
        P(None, "leaf"),
        P(None, "leaf"),
        P("leaf", None),
        P("leaf"),
        P("leaf", None),
        P("leaf", None),
        P(),
    )
    return jax.shard_map(
        per_device, mesh=mesh, in_specs=in_specs, out_specs=P(None, "leaf"), check_vma=False
    )
```

```python
import functools
import math

import jax
import jax.numpy as jnp
from jax import lax
from jax.experimental import pallas as pl
from jax.experimental.pallas import tpu as pltpu
from jax.sharding import PartitionSpec as P


F32 = jnp.float32
BF16 = jnp.bfloat16
AUG = 16
SQ_TOP = 3.0e38
VMEM_MIB = 20
GROUP = 8
NEAR_TILE = 512
CHIP_PARTS = 4
SENDS = {1: (0,), 2: (1,), 3: (2,), 4: (3,)}
SUMS = {
    2: (2, (-1,)),
    3: (3, (-1, 0)),
    4: (4, (-1, 0, 1)),
    5: (12, (-1, 0, 1, 2)),
    6: (4, (-1, 0, 1, 2, 3)),
    7: (None, (-1, 0, 1, 2, 3)),
}


def mm(a, b):
    return lax.dot_general(a, b, (((1,), (0,)), ((), ())), preferred_element_type=F32)


def mm_nt(a, b):
    return lax.dot_general(a, b, (((1,), (1,)), ((), ())), preferred_element_type=F32)


def mm_tn(a, b):
    return lax.dot_general(a, b, (((0,), (0,)), ((), ())), preferred_element_type=F32)


def halves(x):
    high = x.astype(BF16)
    return high, (x - high.astype(F32)).astype(BF16)


def square_rows(pts):
    wide = pts.astype(F32)
    sq = jnp.sum(wide * wide, axis=0, keepdims=True)
    neg = -0.5 * jnp.minimum(sq, SQ_TOP)
    one = neg.astype(BF16).astype(F32)
    rest = neg - one
    two = rest.astype(BF16).astype(F32)
    three = rest - two
    return one, two, three


def aug_rows(pieces, left, width):
    one, two, three = pieces
    row = lax.broadcasted_iota(jnp.int32, (AUG, width), 0)
    if not left:
        row = jnp.where(row < 3, row + 3, jnp.where(row < 6, row - 3, row))
    ones = jnp.where((row >= 3) & (row < 6), 1.0, 0.0)
    body = jnp.where(row == 0, one, jnp.where(row == 1, two, jnp.where(row == 2, three, ones)))
    return body.astype(BF16)


def exp_scaled(z, emb):
    return jnp.exp2(z * (4.0 / emb * math.log2(math.e)))


def affinity(left, right, emb):
    return exp_scaled(mm_tn(left, right), emb)


def left_of(ext, emb):
    return ext[: emb + AUG]


def right_of(ext, emb):
    return jnp.concatenate([ext[:emb], ext[emb + AUG : emb + 2 * AUG]], axis=0)


def one_hot(chosen, pool):
    ids = lax.broadcasted_iota(jnp.int32, (pool, chosen.shape[1]), 0)
    return jnp.where(ids == chosen, 1.0, 0.0).astype(BF16)


def up_kernel(emb, leaf_num, leaf_len, group, all_ref, leaf_skel_ref, local_skel_ref,
              root_ref, leaf_ref, tree_ref, couple_ref, left_ref, node_ref):
    skel_len = leaf_skel_ref.shape[1]
    ext_rows = emb + 2 * AUG

    def leaf_step(step, carry):
        ids = [step * group + k for k in range(group)]
        cols = [pl.ds(pl.multiple_of(leaf * leaf_len, leaf_len), leaf_len) for leaf in ids]
        hots = [one_hot(leaf_skel_ref[pl.ds(leaf, 1), :], leaf_len) for leaf in ids]
        exts = []
        for at in cols:
            pts = all_ref[:emb, at]
            pieces = square_rows(pts)
            exts.append(jnp.concatenate(
                [pts, aug_rows(pieces, True, leaf_len), aug_rows(pieces, False, leaf_len)], axis=0))
        skels = [mm(ext, hot).astype(BF16) for ext, hot in zip(exts, hots)]
        zs = [mm_tn(left_of(skel, emb), right_of(ext, emb)) for skel, ext in zip(skels, exts)]
        lefts = [left_of(ext, emb).T for ext in exts]
        pairs = [halves(exp_scaled(z, emb)) for z in zs]
        charges = [
            (mm_nt(all_ref[emb:, at], high) + mm_nt(all_ref[emb:, at], low)).astype(BF16)
            for at, (high, low) in zip(cols, pairs)
        ]
        for leaf, left, skel, charge, (high, low) in zip(ids, lefts, skels, charges, pairs):
            left_ref[leaf] = left
            node_ref[leaf, :ext_rows, :] = skel
            node_ref[leaf, ext_rows:, :] = charge
            leaf_ref[leaf, :skel_len, :] = high
            leaf_ref[leaf, skel_len:, :] = low
        return carry

    lax.fori_loop(0, leaf_num // group, leaf_step, 0)

    start, row = 0, 0
    width = leaf_num // 2
    while width >= 1:
        part = min(width, group)
        for base in range(0, width, part):
            ks = range(base, base + part)
            hots = [one_hot(local_skel_ref[row + k : row + k + 1, :], 2 * skel_len) for k in ks]
            kids = [(node_ref[start + 2 * k], node_ref[start + 2 * k + 1]) for k in ks]
            exts = [(x[:ext_rows], y[:ext_rows]) for x, y in kids]
            qs = [(x[ext_rows:], y[ext_rows:]) for x, y in kids]
            joins = [jnp.concatenate(pair, axis=1) for pair in exts]
            parents = [mm(joined, hot).astype(BF16) for joined, hot in zip(joins, hots)]
            crosses = [mm_tn(left_of(x, emb), right_of(y, emb)) for x, y in exts]
            zs = [mm_tn(left_of(parent, emb), right_of(joined, emb))
                  for parent, joined in zip(parents, joins)]
            crosses = [halves(exp_scaled(z, emb)) for z in crosses]
            pairs = [halves(exp_scaled(z, emb)) for z in zs]
            parent_qs = []
            for (x, y), (high, low) in zip(qs, pairs):
                joined_q = jnp.concatenate([x, y], axis=1)
                parent_qs.append((mm_nt(joined_q, high) + mm_nt(joined_q, low)).astype(BF16))
            for k, (x, y), (high, low) in zip(ks, qs, crosses):
                couple_ref[row + k, :, :skel_len] = mm_nt(y, high) + mm_nt(y, low)
                couple_ref[row + k, :, skel_len:] = mm(x, high) + mm(x, low)
            for k, parent, parent_q, (high, low) in zip(ks, parents, parent_qs, pairs):
                tree_ref[row + k, :skel_len, :] = high
                tree_ref[row + k, skel_len:, :] = low
                target = start + 2 * width + k
                node_ref[target, :ext_rows, :] = parent
                node_ref[target, ext_rows:, :] = parent_q
        start, row, width = start + 2 * width, row + width, width // 2
    root_ref[...] = node_ref[start]


def level_kernel(emb, cur_ref, sib_ref, chosen_ref, couple_ref, own_ref, next_ref=None):
    skel_len = chosen_ref.shape[1]
    ext_rows = emb + 2 * AUG
    cur, sib = cur_ref[...], sib_ref[...]
    cur_ext, cur_q = cur[:ext_rows], cur[ext_rows:]
    sib_ext, sib_q = sib[:ext_rows], sib[ext_rows:]
    joined = jnp.concatenate([cur_ext, sib_ext], axis=1)
    joined_q = jnp.concatenate([cur_q, sib_q], axis=1)
    hot = one_hot(chosen_ref[...], 2 * skel_len)
    parent = mm(joined, hot).astype(BF16)
    high, low = halves(affinity(left_of(parent, emb), right_of(joined, emb), emb))
    if next_ref is not None:
        next_ref[:ext_rows, :] = parent
        next_ref[ext_rows:, :] = (mm_nt(joined_q, high) + mm_nt(joined_q, low)).astype(BF16)
    own_ref[:skel_len, :] = high[:, :skel_len]
    own_ref[skel_len:, :] = low[:, :skel_len]
    high, low = halves(affinity(left_of(sib_ext, emb), right_of(cur_ext, emb), emb))
    couple_ref[...] = mm(sib_q, high) + mm(sib_q, low)


def near_sum(leaf_len, bucket, first, last, lists_ref, left_ref, pts_ref, prb_ref, out_ref):
    tile = min(NEAR_TILE, leaf_len)
    emb = pts_ref.shape[0]

    def step(item, carry):
        leaf = lists_ref[2 * bucket, item]
        place = lists_ref[2 * bucket + 1, item]
        cols = pl.ds(pl.multiple_of(place * leaf_len, leaf_len), leaf_len)
        pts = pts_ref[:, cols]
        right = jnp.concatenate([pts, aug_rows(square_rows(pts), False, leaf_len)], axis=0)
        prb = prb_ref[:, cols]
        starts = list(range(0, leaf_len, tile))
        terms, ahead, kern = [], mm(left_ref[leaf, :tile, :], right), None
        for n in range(len(starts)):
            z = ahead
            if n + 1 < len(starts):
                ahead = mm(left_ref[leaf, starts[n + 1] : starts[n + 1] + tile, :], right)
            last, kern = kern, exp_scaled(z, emb).astype(BF16)
            if n > 0:
                terms.append(mm_nt(prb, last))
        terms.append(mm_nt(prb, kern))
        at = pl.ds(pl.multiple_of(leaf * leaf_len, leaf_len), leaf_len)
        out_ref[:, at] += jnp.concatenate(terms, axis=1)
        return carry

    lax.fori_loop(first, last, step, 0)


def near_own_kernel(emb, leaf_len, chip_span, ids_ref, count_ref, left_ref, all_ref,
                    out_ref, lists_ref):
    leaf_num = count_ref.shape[0]
    bucket_num = lists_ref.shape[0] // 2
    unused, lengths = bucket_num - 1, 2 * bucket_num
    out_ref[...] = jnp.zeros_like(out_ref)
    for bucket in range(bucket_num):
        lists_ref[lengths, bucket] = 0

    def scan_leaf(leaf, carry):
        count = count_ref[leaf]
        for slot in range(ids_ref.shape[1]):
            source = ids_ref[leaf, slot]
            on_link = source < leaf_num
            on_chip = source >= 2 * leaf_num
            home = source - jnp.where(on_link, 0, jnp.where(on_chip, 2 * leaf_num, leaf_num))
            part = jnp.where(on_chip, lax.div(home, chip_span), 0)
            bucket = jnp.where(on_link, 1, jnp.where(on_chip, 2 + part, 0))
            bucket = jnp.where(slot < count, bucket, unused)
            filled = lists_ref[lengths, bucket]
            lists_ref[2 * bucket, filled] = leaf
            lists_ref[2 * bucket + 1, filled] = home - part * chip_span
            lists_ref[lengths, bucket] = filled + 1
        return carry

    lax.fori_loop(0, leaf_num, scan_leaf, 0, unroll=4)
    near_sum(leaf_len, 0, 0, lists_ref[lengths, 0], lists_ref, left_ref,
             all_ref.at[:emb], all_ref.at[emb:], out_ref)


def near_kernel(emb, leaf_len, turns, lists_ref, left_ref, *refs):
    _, out_ref = refs[-2:]
    lengths = lists_ref.shape[0] - 1
    done = {}
    for turn, (budget, buckets) in enumerate(turns):
        for bucket, src_ref in zip(buckets, refs[:-2]):
            first = done.get(bucket, 0)
            count = lists_ref[lengths, bucket] - first
            if budget is not None:
                count = jnp.minimum(count, budget)
                budget = budget - count
            done[bucket] = first + count
            if turn + 1 == len(turns):
                near_sum(leaf_len, bucket, first, first + count, lists_ref, left_ref,
                         src_ref.at[:emb], src_ref.at[emb:], out_ref)


def down_kernel(leaf_num, leaf_len, level_num, *refs):
    owns, couples = refs[:level_num], refs[level_num : 2 * level_num]
    tree_ref, tree_couple_ref, leaf_ref, near_ref, out_ref, field_ref = refs[2 * level_num :]
    skel_len = tree_ref.shape[1] // 2
    probe_num = out_ref.shape[0]

    def spread(field, high, low):
        field_high, field_low = halves(field)
        both = mm(jnp.concatenate([field_high, field_low], axis=0), high)
        return both[:probe_num] + both[probe_num:] + mm(field_high, low)

    field = jnp.zeros((probe_num, skel_len), F32)
    for own, couple in zip(reversed(owns), reversed(couples)):
        field = spread(field, own[:skel_len], own[skel_len:]) + couple[...]

    fields, row = [field], leaf_num - 2
    while len(fields) < leaf_num:
        below = []
        for k, field in enumerate(fields):
            both = spread(field, tree_ref[row + k, :skel_len, :],
                          tree_ref[row + k, skel_len:, :]) + tree_couple_ref[row + k]
            below += [both[:, :skel_len], both[:, skel_len:]]
        fields, row = below, row - len(below)
    for leaf, field in enumerate(fields):
        field_ref[leaf] = field

    for leaf in range(leaf_num):
        far = spread(field_ref[leaf], leaf_ref[leaf, :skel_len, :], leaf_ref[leaf, skel_len:, :])
        cols = slice(leaf * leaf_len, (leaf + 1) * leaf_len)
        out_ref[:, cols] = near_ref[:, cols] + far


def whole(num):
    return [pl.BlockSpec(memory_space=pltpu.VMEM)] * num


def params():
    return pltpu.CompilerParams(vmem_limit_bytes=VMEM_MIB * 1024 * 1024)


def cost(flops, read):
    return pl.CostEstimate(flops=flops, bytes_accessed=read, transcendentals=0)


def across_link(block, axis):
    count = lax.axis_size(axis)
    route = [(i, i + 1) for i in range(1, count - 1, 2)]
    return lax.ppermute(block, axis, route + [(j, i) for i, j in route])


def partner(block, axis, stride):
    count = lax.axis_size(axis)
    return lax.ppermute(block, axis, [(i, i ^ (1 << stride)) for i in range(count)])


def per_device(points, probes, near_list, near_count, leaf_skel, local_skel, upper_skel):
    emb, shard_len = points.shape
    leaf_num, slot_num = near_list.shape
    leaf_len = shard_len // leaf_num
    skel_len = leaf_skel.shape[1]
    probe_num = probes.shape[0]
    me = lax.axis_index("leaf")
    dev_num = lax.axis_size("leaf")
    level_num = dev_num.bit_length() - 1
    node_rows = emb + 2 * AUG + probe_num
    node_total = 2 * leaf_num - 1

    chip_span = leaf_num // CHIP_PARTS

    joined = jnp.concatenate([points, probes], axis=0)
    link = across_link(joined, "leaf")

    relative = near_list - (me * leaf_num - leaf_num)
    odd = (me & 1) == 1
    relative = jnp.where(
        odd & (relative < leaf_num), relative + 2 * leaf_num,
        jnp.where(odd & (relative >= 2 * leaf_num), relative - 2 * leaf_num, relative))
    bits = jnp.arange(level_num, dtype=jnp.int32)
    rows = dev_num - (dev_num >> bits) + (me >> (bits + 1))
    chosen = jnp.take(upper_skel, rows, axis=0) ^ (((me >> bits) & 1) * skel_len)[:, None]

    sd = jax.ShapeDtypeStruct
    cur, leaf_kern, tree, tree_couple, left = pl.pallas_call(
        functools.partial(up_kernel, emb, leaf_num, leaf_len, GROUP),
        out_shape=(
            sd((node_rows, skel_len), BF16),
            sd((leaf_num, 2 * skel_len, leaf_len), BF16),
            sd((leaf_num - 1, 2 * skel_len, 2 * skel_len), BF16),
            sd((leaf_num - 1, probe_num, 2 * skel_len), F32),
            sd((leaf_num, leaf_len, emb + AUG), BF16),
        ),
        in_specs=whole(3),
        out_specs=tuple(whole(5)),
        scratch_shapes=[pltpu.VMEM((node_total, node_rows, skel_len), BF16)],
        compiler_params=params(),
        cost_estimate=cost(5_000_000_000, 4_000_000),
        name="up",
    )(joined, leaf_skel, local_skel)

    bucket_num = 3 + CHIP_PARTS
    smem = [pl.BlockSpec(memory_space=pltpu.SMEM)]
    near, lists = pl.pallas_call(
        functools.partial(near_own_kernel, emb, leaf_len, chip_span),
        out_shape=(
            sd((probe_num, shard_len), F32),
            sd((2 * bucket_num + 1, leaf_num * slot_num), jnp.int32),
        ),
        in_specs=smem * 2 + whole(2),
        out_specs=tuple(whole(1) + smem),
        compiler_params=params(),
        cost_estimate=cost(5_000_000_000, 4_000_000),
        name="near_own",
    )(relative, near_count, left, joined)

    def near_call(near, turns, sources):
        return pl.pallas_call(
            functools.partial(near_kernel, emb, leaf_len, turns),
            out_shape=sd(near.shape, F32),
            in_specs=smem + whole(2 + len(sources)),
            out_specs=whole(1)[0],
            input_output_aliases={2 + len(sources): 0},
            compiler_params=params(),
            cost_estimate=cost(1_000_000_000, 1_000_000),
            name="near_beside",
        )(lists, left, *sources, near)

    chip_wide = chip_span * leaf_len
    parts = [joined[:, k * chip_wide : (k + 1) * chip_wide] for k in range(CHIP_PARTS)]
    cur, near, chosen, parts = lax.optimization_barrier((cur, near, chosen, parts))
    arrived, turns = {-1: link}, ()

    owns, couples = [], []
    for level in range(level_num):
        sib = partner(cur, "leaf", level)
        for k in SENDS.get(level, ()):
            part, cur = lax.optimization_barrier((parts[k], cur))
            arrived[k] = partner(part, "leaf", 0)
        if level in SUMS:
            budget, ks = SUMS[level]
            turns += ((budget, tuple(2 + k for k in ks)),)
            cur, near = lax.optimization_barrier((cur, near))
            near = near_call(near, turns, [arrived[k] for k in ks])
            sib, near = lax.optimization_barrier((sib, near))
        more = 1 if level + 1 < level_num else 0
        couple, own, *rest = pl.pallas_call(
            functools.partial(level_kernel, emb),
            out_shape=(
                sd((probe_num, skel_len), F32),
                sd((2 * skel_len, skel_len), BF16),
            ) + (sd((node_rows, skel_len), BF16),) * more,
            in_specs=whole(3),
            out_specs=tuple(whole(2 + more)),
            compiler_params=params(),
            cost_estimate=cost(1_000_000_000, 200_000),
            name="level",
        )(cur, sib, chosen[level : level + 1])
        if rest:
            cur = rest[0]
        owns.append(own)
        couples.append(couple)

    return pl.pallas_call(
        functools.partial(down_kernel, leaf_num, leaf_len, level_num),
        out_shape=sd((probe_num, shard_len), F32),
        in_specs=whole(2 * level_num + 4),
        out_specs=whole(1)[0],
        scratch_shapes=[pltpu.VMEM((leaf_num, probe_num, skel_len), F32)],
        compiler_params=params(),
        cost_estimate=cost(5_000_000_000, 4_000_000),
        name="down",
    )(*owns, *couples, tree, tree_couple, leaf_kern, near)


def solution(mesh):
    in_specs = (
        P(None, "leaf"),
        P(None, "leaf"),
        P("leaf", None),
        P("leaf"),
        P("leaf", None),
        P("leaf", None),
        P(),
    )
    return jax.shard_map(
        per_device, mesh=mesh, in_specs=in_specs, out_specs=P(None, "leaf"), check_vma=False
    )
```
